32 devices in a mesh: rep: 4 (over y, x), fsdp: 8 (over z, core).
Axes of the slice: x: 2, y: 2, z: 4, core: 2. Of those that a mesh axis runs over, the one named last changes fastest.
Arguments:
- patches: bfloat16 [128, 128, 1024], P(('rep', 'fsdp')), may hold values from -6 to 6
- enc_gain1: bfloat16 [1024], P('fsdp'), may hold values from 0.5 to 1.5
- enc_qkv: bfloat16 [1024, 3072], P('fsdp'), may hold values from -0.1875 to 0.1875
- enc_proj: bfloat16 [1024, 1024], P('fsdp'), may hold values from -1.5 to 1.5
- enc_gain2: bfloat16 [1024], P('fsdp'), may hold values from 0.5 to 1.5
- enc_up: bfloat16 [1024, 4096], P('fsdp'), may hold values from -0.1875 to 0.1875
- enc_down: bfloat16 [4096, 1024], P('fsdp'), may hold values from -0.09375 to 0.09375
- embed_w: bfloat16 [1024, 512], P('fsdp'), may hold values from -0.1875 to 0.1875
- mask_token: bfloat16 [512], P('fsdp'), may hold values from -6 to 6
- dec_gain1: bfloat16 [512], P('fsdp'), may hold values from 0.5 to 1.5
- dec_qkv: bfloat16 [512, 1536], P('fsdp'), may hold values from -0.25 to 0.25
- dec_proj: bfloat16 [512, 512], P('fsdp'), may hold values from -2 to 2
- dec_gain2: bfloat16 [512], P('fsdp'), may hold values from 0.5 to 1.5
- dec_up: bfloat16 [512, 2048], P('fsdp'), may hold values from -0.25 to 0.25
- dec_down: bfloat16 [2048, 512], P('fsdp'), may hold values from -0.125 to 0.125
- visible: int32 [128], P(('rep', 'fsdp')), may hold values from 64 to 128, as said below
- unshuffle: int32 [128, 256], P(('rep', 'fsdp')), may hold values from 0 to 255, each once within a row
- ground_dist: float32 [128], P(('rep', 'fsdp')), may hold values from 0.5 to 2
- cotangent: bfloat16 [128, 256, 512], P(('rep', 'fsdp')), may hold values from -6 to 6
Outputs:
- enc_out: bfloat16 [128, 128, 1024], P(('rep', 'fsdp'))
- dec_out: bfloat16 [128, 256, 512], P(('rep', 'fsdp'))
- patches_grad: bfloat16 [128, 128, 1024], P(('rep', 'fsdp'))
- grad_enc_gain1: float32 [1024], P('fsdp')
- grad_enc_qkv: float32 [1024, 3072], P('fsdp')
- grad_enc_proj: float32 [1024, 1024], P('fsdp')
- grad_enc_gain2: float32 [1024], P('fsdp')
- grad_enc_up: float32 [1024, 4096], P('fsdp')
- grad_enc_down: float32 [4096, 1024], P('fsdp')
- grad_embed: float32 [1024, 512], P('fsdp')
- grad_mask: float32 [512], P('fsdp')
- grad_dec_gain1: float32 [512], P('fsdp')
- grad_dec_qkv: float32 [512, 1536], P('fsdp')
- grad_dec_proj: float32 [512, 512], P('fsdp')
- grad_dec_gain2: float32 [512], P('fsdp')
- grad_dec_up: float32 [512, 2048], P('fsdp')
- grad_dec_down: float32 [2048, 512], P('fsdp')
The draws below stay inside these ranges and needn't reach their ends.
Inputs may be any that keep to these rules, and one draw needn't show every extreme that they name: The first visible[i] encoder slots of image i are live, the rest are padding; some image has 128 live slots and some 128 // 2. `unshuffle`: each row is a permutation of 0 to 255.
All inputs are finite; a program needn't handle non-finite values.
Results may differ from the reference program's by a relative error of at most 0.024.
Values may be sent and summed in bfloat16 or wider, within the bound.
A program may use at most 256 MiB of HBM per device.

```python
import math
import jax
import jax.numpy as jnp
from jax import lax

D = 1024
HEADS = 16
FF = 4096
DD = 512
HEADS_D = 16
FFD = 2048
GRID = 16
VIS = 128
PATCHES = 256
IMAGES = 128


def draw_visible(key, part):
    key_counts, key_place = jax.random.split(key)
    counts = jax.random.randint(key_counts, (IMAGES,), VIS // 2, VIS + 1, dtype=jnp.int32)
    place = jax.random.randint(key_place, (), 0, IMAGES, dtype=jnp.int32)
    counts = counts.at[place].set(VIS)
    other_place = (place + IMAGES // 2) % IMAGES
    return counts.at[other_place].set(VIS // 2)


def block_levels(key, dims, shards, low, largest):
    def one(position, shards_of):
        steps = jax.random.uniform(jax.random.fold_in(jax.random.fold_in(key, 6), position), (shards_of,), jnp.float32, low / len(shards), largest / len(shards))
        return jnp.repeat(jnp.exp(steps), dims[position] // shards_of).reshape((-1,) + (1,) * (len(dims) - position - 1))

    factor_of = one(*shards[0])
    for cut in shards[1:]:
        factor_of = factor_of * one(*cut)
    return factor_of


def normal_values(own_key, extent, scale, bound, cuts=(), kind=jnp.bfloat16):
    factor_of = block_levels(own_key, extent, cuts, -0.22, 0.18) if cuts else 1.0
    entries = jax.random.normal(own_key, extent, jnp.float32) * scale * factor_of
    return jnp.minimum(jnp.maximum(entries, -bound), bound).astype(kind)


def setup_inputs(seed: int = 0) -> dict:
    splits = jax.random.split(jax.random.key(seed), 20)
    patches = normal_values(splits[0], (IMAGES, VIS, D), 1.0, 6.0, ((0, 32),))
    enc_gain1 = jnp.clip(1.0 + 0.1 * jax.random.normal(splits[1], (D,), jnp.float32), 0.5, 1.5).astype(jnp.bfloat16)
    enc_qkv = normal_values(splits[2], (D, 3 * D), D ** -0.5, 0.1875, ((0, 8),))
    enc_proj = normal_values(splits[3], (D, D), (max(D // 64, 1)) ** -0.5, 1.5, ((0, 8),))
    enc_gain2 = jnp.clip(1.0 + 0.1 * jax.random.normal(splits[4], (D,), jnp.float32), 0.5, 1.5).astype(jnp.bfloat16)
    enc_up = normal_values(splits[5], (D, FF), D ** -0.5, 0.1875, ((0, 8),))
    enc_down = normal_values(splits[6], (FF, D), FF ** -0.5, 0.09375, ((0, 8),))
    embed_w = normal_values(splits[7], (D, DD), D ** -0.5, 0.1875, ((0, 8),))
    mask_token = normal_values(splits[8], (DD,), 1.0, 6.0, ((0, 8),))
    dec_gain1 = jnp.clip(1.0 + 0.1 * jax.random.normal(splits[9], (DD,), jnp.float32), 0.5, 1.5).astype(jnp.bfloat16)
    dec_qkv = normal_values(splits[10], (DD, 3 * DD), DD ** -0.5, 0.25, ((0, 8),))
    dec_proj = normal_values(splits[11], (DD, DD), (max(DD // 64, 1)) ** -0.5, 2.0, ((0, 8),))
    dec_gain2 = jnp.clip(1.0 + 0.1 * jax.random.normal(splits[12], (DD,), jnp.float32), 0.5, 1.5).astype(jnp.bfloat16)
    dec_up = normal_values(splits[13], (DD, FFD), DD ** -0.5, 0.25, ((0, 8),))
    dec_down = normal_values(splits[14], (FFD, DD), FFD ** -0.5, 0.125, ((0, 8),))
    visible = draw_visible(jax.random.fold_in(splits[19], 71), 0)
    unshuffle = jax.vmap(lambda own: jax.random.permutation(own, PATCHES))(jax.random.split(splits[16], IMAGES)).reshape((IMAGES, PATCHES)).astype(jnp.int32)
    ground_dist = jnp.clip(jnp.exp(math.log(2.0) - 1.3862944 * jax.random.uniform(splits[17], (IMAGES,), jnp.float32) ** block_levels(splits[17], (IMAGES,), ((0, 32),), -0.2, 0.2)), 0.5, 2.0)
    cotangent = normal_values(splits[18], (IMAGES, PATCHES, DD), 1.0, 6.0, ((0, 32),))
    return {"patches": patches, "enc_gain1": enc_gain1, "enc_qkv": enc_qkv, "enc_proj": enc_proj, "enc_gain2": enc_gain2, "enc_up": enc_up, "enc_down": enc_down, "embed_w": embed_w, "mask_token": mask_token, "dec_gain1": dec_gain1, "dec_qkv": dec_qkv, "dec_proj": dec_proj, "dec_gain2": dec_gain2, "dec_up": dec_up, "dec_down": dec_down, "visible": visible, "unshuffle": unshuffle, "ground_dist": ground_dist, "cotangent": cotangent}


@jax.custom_vjp
def low(v):
    return lax.optimization_barrier(v.astype(jnp.bfloat16)).astype(jnp.float32)

@jax.custom_vjp
def low_back(v):
    return v

def low_keep(v):
    return (low(v), None)

def low_pass(kept, grad):
    return (grad,)

def back_keep(v):
    return (v, None)

def back_low(kept, grad):
    return (low(grad),)
low.defvjp(low_keep, low_pass)
low_back.defvjp(back_keep, back_low)
norm_epsilon = 1e-06

def exact_dot(left, right):
    return jnp.dot(left, right, precision=lax.Precision.HIGHEST, preferred_element_type=jnp.float32)

def norm_stats(values):
    centre = values - lax.optimization_barrier(jnp.mean(values, axis=-1, keepdims=True))
    return centre * lax.rsqrt(lax.optimization_barrier(jnp.mean(centre * centre, axis=-1, keepdims=True)) + norm_epsilon)

def position_table(distance, grid_side, model_width):
    quarter = model_width // 4
    frequency = 1.0 / 10000.0 ** (jnp.arange(quarter, dtype=jnp.float32) / quarter)
    places = jnp.arange(grid_side * grid_side, dtype=jnp.int32)
    column = (places % grid_side).astype(jnp.float32)
    row_pos = (places // grid_side).astype(jnp.float32)
    along_c = distance[:, None, None] * column[None, :, None] * frequency[None, None, :]
    along_r = distance[:, None, None] * row_pos[None, :, None] * frequency[None, None, :]
    return jnp.concatenate([jnp.sin(along_c), jnp.cos(along_c), jnp.sin(along_r), jnp.cos(along_r)], axis=-1)

def block_forward(rows, weights, live, head_count, images, length):
    gain_one, w_qkv, w_out, gain_two, w_up, w_down = weights
    model_width = rows.shape[-1]
    head_size = model_width // head_count
    score_scale = head_size ** (-0.5)
    normed_one = low(norm_stats(rows) * gain_one)
    packed = low(low_back(exact_dot(normed_one, w_qkv))).reshape(images, length, 3, head_count, head_size)
    queries, key_rows, value_rows = (packed[:, :, 0], packed[:, :, 1], packed[:, :, 2])
    raw_scores = jnp.einsum('nqhd,nkhd->nhqk', queries, key_rows, precision=lax.Precision.HIGHEST) * score_scale
    valid = jnp.arange(length, dtype=jnp.int32)[None, None, None, :] < live[:, None, None, None]
    scores = low_back(jnp.where(valid, raw_scores, -1e+30))
    highest = lax.optimization_barrier(jnp.max(scores, axis=-1, keepdims=True))
    exponent = jnp.exp(scores - highest)
    soft_weights = low(exponent / lax.optimization_barrier(jnp.sum(exponent, axis=-1, keepdims=True)))
    mixed_rows = low(low_back(jnp.einsum('nhqk,nkhd->nqhd', soft_weights, value_rows, precision=lax.Precision.HIGHEST)))
    middle = rows + low_back(exact_dot(mixed_rows.reshape(images * length, model_width), w_out))
    normed_two = low(norm_stats(middle) * gain_two)
    hidden = low(jax.nn.gelu(low_back(exact_dot(normed_two, w_up)), approximate=False))
    return middle + low_back(exact_dot(hidden, w_down))

def reference(patches, enc_gain1, enc_qkv, enc_proj, enc_gain2, enc_up, enc_down, embed_w, mask_token, dec_gain1, dec_qkv, dec_proj, dec_gain2, dec_up, dec_down, visible, unshuffle, ground_dist, cotangent):
    params = tuple((member.astype(jnp.float32) for member in (enc_gain1, enc_qkv, enc_proj, enc_gain2, enc_up, enc_down, embed_w, mask_token, dec_gain1, dec_qkv, dec_proj, dec_gain2, dec_up, dec_down)))
    group_size = math.gcd(IMAGES, 16)
    group_count = IMAGES // group_size

    def forward(weights_all, inputs):
        enc_weights = weights_all[0:6]
        embed_weight = weights_all[6]
        mask_vector = weights_all[7]
        dec_weights = weights_all[8:14]

        def one_group(group_items):
            group_in, group_live, group_order, group_dist = group_items
            enc_rows = block_forward(group_in.reshape(group_size * VIS, D), enc_weights, group_live, HEADS, group_size, VIS)
            enc_low = low(enc_rows)
            embedded = low_back(exact_dot(enc_low, embed_weight)).reshape(group_size, VIS, DD)
            picked = jnp.take_along_axis(embedded, jnp.minimum(group_order, VIS - 1)[:, :, None], axis=1)
            shown_rows = (group_order < group_live[:, None])[:, :, None]
            dec_in = jnp.where(shown_rows, picked, mask_vector[None, None, :]) + position_table(group_dist, GRID, DD)
            all_live = jnp.full((group_size,), PATCHES, jnp.int32)
            dec_rows = block_forward(dec_in.reshape(group_size * PATCHES, DD), dec_weights, all_live, HEADS_D, group_size, PATCHES)
            return (dec_rows.reshape(group_size, PATCHES, DD), enc_rows.reshape(group_size, VIS, D))
        group_items = (inputs.reshape(group_count, group_size, VIS, D), visible.reshape(group_count, group_size), unshuffle.reshape(group_count, group_size, PATCHES), ground_dist.reshape(group_count, group_size))
        dec_all, enc_all = lax.map(jax.checkpoint(one_group), group_items)
        return (dec_all.reshape(IMAGES, PATCHES, DD), enc_all.reshape(IMAGES, VIS, D))
    dec_result, pullback, enc_result = jax.vjp(forward, params, patches.astype(jnp.float32), has_aux=True)
    weight_grads, d_patches = pullback(cotangent.astype(jnp.float32))
    return (enc_result.astype(jnp.bfloat16), dec_result.astype(jnp.bfloat16), d_patches.astype(jnp.bfloat16), weight_grads[0], weight_grads[1], weight_grads[2], weight_grads[3], weight_grads[4], weight_grads[5], weight_grads[6], weight_grads[7], weight_grads[8], weight_grads[9], weight_grads[10], weight_grads[11], weight_grads[12], weight_grads[13])
```

```python
import functools
import math

import jax
import jax.numpy as jnp
from jax import lax
from jax.experimental import pallas as pl
from jax.experimental.pallas import tpu as pltpu
from jax.sharding import PartitionSpec as P

HEADS = 16
HEADS_D = 16
GRID = 16


norm_epsilon = 1e-06


def matmul(left, right):
    return jnp.dot(left, right, preferred_element_type=jnp.float32)


def matmul_tn(left, right):
    return lax.dot_general(
        left, right, (((0,), (0,)), ((), ())), preferred_element_type=jnp.float32
    )


def matmul_nt(left, right):
    return lax.dot_general(
        left, right, (((1,), (1,)), ((), ())), preferred_element_type=jnp.float32
    )


def norm_stats(values):
    centre = values - jnp.mean(values, axis=-1, keepdims=True)
    inv_dev = lax.rsqrt(jnp.mean(centre * centre, axis=-1, keepdims=True) + norm_epsilon)
    return (centre * inv_dev, inv_dev)


def norm_back(d_scaled, normal, inv_dev):
    return inv_dev * (
        d_scaled
        - jnp.mean(d_scaled, axis=-1, keepdims=True)
        - normal * jnp.mean(d_scaled * normal, axis=-1, keepdims=True)
    )


def position_table(distance, grid_side, model_width):
    quarter = model_width // 4
    frequency = 1.0 / 10000.0 ** (jnp.arange(quarter, dtype=jnp.float32) / quarter)
    places = jnp.arange(grid_side * grid_side, dtype=jnp.int32)
    column = (places % grid_side).astype(jnp.float32)
    row_pos = (places // grid_side).astype(jnp.float32)
    along_c = distance[:, None, None] * column[None, :, None] * frequency[None, None, :]
    along_r = distance[:, None, None] * row_pos[None, :, None] * frequency[None, None, :]
    return jnp.concatenate(
        [jnp.sin(along_c), jnp.cos(along_c), jnp.sin(along_r), jnp.cos(along_r)], axis=-1
    )


def by_groups(function, members, length):
    images = members[0].shape[0]
    per_step = math.gcd(images, max(1, 512 // length))
    shaped = tuple(
        (member.reshape((images // per_step, per_step) + member.shape[1:]) for member in members)
    )
    results = lax.map(lambda group_items: function(*group_items), shaped)
    return jax.tree.map(lambda result: result.reshape((images,) + result.shape[2:]), results)


def masked_scores(queries, key_rows, live, score_scale):
    raw_scores = (
        jnp.einsum("nqhd,nkhd->nhqk", queries, key_rows, preferred_element_type=jnp.float32)
        * score_scale
    )
    length = key_rows.shape[1]
    valid = jnp.arange(length, dtype=jnp.int32)[None, None, None, :] < live[:, None, None, None]
    return jnp.where(valid, raw_scores, -1e30)


def split_heads(packed, head_count):
    images, length, three_width = packed.shape
    split_parts = packed.reshape(images, length, 3, head_count, three_width // (3 * head_count))
    return (split_parts[:, :, 0], split_parts[:, :, 1], split_parts[:, :, 2])


def attend_group(packed, live, head_count, score_scale):
    queries, key_rows, value_rows = split_heads(packed, head_count)
    scores = masked_scores(queries, key_rows, live, score_scale)
    highest = jnp.max(scores, axis=-1, keepdims=True)
    exponent = jnp.exp(scores - highest)
    summed = jnp.sum(exponent, axis=-1, keepdims=True)
    soft_weights = (exponent / summed).astype(jnp.bfloat16)
    mixed_rows = jnp.einsum(
        "nhqk,nkhd->nqhd", soft_weights, value_rows, preferred_element_type=jnp.float32
    )
    images, length = (packed.shape[0], packed.shape[1])
    log_total = (highest + jnp.log(summed))[..., 0]
    return (
        mixed_rows.reshape(images, length, packed.shape[2] // 3).astype(jnp.bfloat16),
        log_total,
    )


def attend_back_group(packed, log_total, d_mixed, live, head_count, score_scale):
    queries, key_rows, value_rows = split_heads(packed, head_count)
    scores = masked_scores(queries, key_rows, live, score_scale)
    soft_float = jnp.exp(scores - log_total[..., None])
    d_heads = d_mixed.reshape(queries.shape)
    d_soft = jnp.einsum("nqhd,nkhd->nhqk", d_heads, value_rows, preferred_element_type=jnp.float32)
    row_dot = jnp.sum(soft_float * d_soft, axis=-1, keepdims=True)
    d_scores = (soft_float * (d_soft - row_dot)).astype(jnp.bfloat16)
    d_queries = (
        jnp.einsum("nhqk,nkhd->nqhd", d_scores, key_rows, preferred_element_type=jnp.float32)
        * score_scale
    )
    d_keys = (
        jnp.einsum("nhqk,nqhd->nkhd", d_scores, queries, preferred_element_type=jnp.float32)
        * score_scale
    )
    d_values = jnp.einsum(
        "nhqk,nqhd->nkhd",
        soft_float.astype(jnp.bfloat16),
        d_heads,
        preferred_element_type=jnp.float32,
    )
    stacked = jnp.stack([d_queries, d_keys, d_values], axis=2)
    return stacked.reshape(packed.shape).astype(jnp.bfloat16)


def block_forward(rows, weights, live, head_count, images, length):
    gain_one, w_qkv, w_out, gain_two, w_up, w_down = weights
    model_width = rows.shape[-1]
    score_scale = (model_width // head_count) ** (-0.5)
    normal_one, inv_one = norm_stats(rows)
    normed_one = (normal_one * gain_one).astype(jnp.bfloat16)
    packed = matmul(normed_one, w_qkv).astype(jnp.bfloat16).reshape(images, length, 3 * model_width)

    def attend(group_packed, group_live):
        return attend_group(group_packed, group_live, head_count, score_scale)

    mixed_rows, log_total = by_groups(attend, (packed, live), length)
    middle = rows + matmul(mixed_rows.reshape(images * length, model_width), w_out)
    normal_two, inv_two = norm_stats(middle)
    normed_two = (normal_two * gain_two).astype(jnp.bfloat16)
    hidden = jax.nn.gelu(matmul(normed_two, w_up), approximate=False).astype(jnp.bfloat16)
    return (middle + matmul(hidden, w_down), (rows, packed, mixed_rows, log_total, middle))


def block_backward(kept_state, d_out, weights, live, head_count, images, length):
    rows, packed, mixed_rows, log_total, middle = kept_state
    gain_one, w_qkv, w_out, gain_two, w_up, w_down = weights
    model_width = rows.shape[-1]
    score_scale = (model_width // head_count) ** (-0.5)
    normal_two, inv_two = norm_stats(middle)
    normed_two = (normal_two * gain_two).astype(jnp.bfloat16)
    up_proj = matmul(normed_two, w_up)
    hidden_float, gelu_back = jax.vjp(lambda inner: jax.nn.gelu(inner, approximate=False), up_proj)
    hidden = hidden_float.astype(jnp.bfloat16)
    d_branch = d_out.astype(jnp.bfloat16)
    grad_down = matmul_tn(hidden, d_branch)
    d_hidden = matmul_nt(d_branch, w_down)
    d_up = gelu_back(d_hidden)[0].astype(jnp.bfloat16)
    grad_up = matmul_tn(normed_two, d_up)
    d_normed_two = matmul_nt(d_up, w_up)
    grad_gain_two = jnp.sum(d_normed_two * normal_two, axis=0)
    d_middle = d_out + norm_back(d_normed_two * gain_two, normal_two, inv_two)
    d_attn = d_middle.astype(jnp.bfloat16)
    grad_out = matmul_tn(mixed_rows.reshape(images * length, model_width), d_attn)
    d_mixed = matmul_nt(d_attn, w_out).astype(jnp.bfloat16).reshape(images, length, model_width)

    def attend_back(group_packed, group_total, group_grad, group_live):
        return attend_back_group(
            group_packed, group_total, group_grad, group_live, head_count, score_scale
        )

    d_packed = by_groups(attend_back, (packed, log_total, d_mixed, live), length)
    d_packed = d_packed.reshape(images * length, 3 * model_width)
    normal_one, inv_one = norm_stats(rows)
    normed_one = (normal_one * gain_one).astype(jnp.bfloat16)
    grad_qkv = matmul_tn(normed_one, d_packed)
    d_normed_one = matmul_nt(d_packed, w_qkv)
    grad_gain_one = jnp.sum(d_normed_one * normal_one, axis=0)
    d_rows = d_middle + norm_back(d_normed_one * gain_one, normal_one, inv_one)
    return (d_rows, (grad_gain_one, grad_qkv, grad_out, grad_gain_two, grad_up, grad_down))


MESH_ID = pl.DeviceIdType.MESH


def places():
    rep = lax.axis_index("rep")
    own = lax.axis_index("fsdp")
    return rep, own, own // 2, own % 2


def dev(rep, own):
    return {"rep": rep, "fsdp": own}


def greet(rep, own, line, length):
    barrier = pltpu.get_barrier_semaphore()

    def call(r, f):
        pl.semaphore_signal(barrier, inc=1, device_id=dev(r, f), device_id_type=MESH_ID)

    call(rep, own + 1 - 2 * (own % 2))
    call(rep + 1 - 2 * (rep % 2), own)
    call((rep + 2) % 4, own)

    @pl.when(line > 0)
    def _():
        call(rep, own - 2)

    @pl.when(line < length - 1)
    def _():
        call(rep, own + 2)

    ends = (line == 0).astype(jnp.int32) + (line == length - 1).astype(jnp.int32)
    pl.semaphore_wait(barrier, 5 - ends)


def gather_kernel(shapes, length, *refs):
    count = len(shapes)
    ins, outs, rest = (refs[:count], refs[count : 2 * count], refs[2 * count :])
    (own_sem, q_send, q_recv, o_send, z_send, z_recv, x_send, x_recv, y_send, y_recv) = rest[:10]
    d_send, d_recv, p_send, p_recv = rest[10:]
    rep, own, line, core = places()
    x_peer, y_peer = (rep + 1 - 2 * (rep % 2), (rep + 2) % 4)
    mate = own + 1 - 2 * core
    greet(rep, own, line, length)

    def window(k, source, quarter):
        rows, cols = shapes[k]
        start = pl.multiple_of((2 * source + core) * rows, 16)
        if quarter is None:
            return outs[k].at[pl.ds(start, rows), :]
        return outs[k].at[
            pl.ds(start, rows), pl.ds(pl.multiple_of(quarter * (cols // 4), 128), cols // 4)
        ]

    def send(src, dst, s_sem, r_sem, r, f):
        return pltpu.make_async_remote_copy(
            src_ref=src, dst_ref=dst, send_sem=s_sem, recv_sem=r_sem,
            device_id=dev(r, f), device_id_type=MESH_ID,
        )

    def mine(k):
        _, cols = shapes[k]
        return ins[k].at[:, pl.ds(pl.multiple_of(rep * (cols // 4), 128), cols // 4)]

    def left(k):
        return send(mine(k), window(k, line, rep), o_send.at[k, 0], z_recv.at[k, line], rep, own - 2)

    def right(k):
        return send(mine(k), window(k, line, rep), o_send.at[k, 1], z_recv.at[k, line], rep, own + 2)

    def start_own(k):
        @pl.when(line > 0)
        def _():
            left(k).start()

        @pl.when(line < length - 1)
        def _():
            right(k).start()

    def local(k):
        rows, _ = shapes[k]
        return pltpu.make_async_copy(
            ins[k], outs[k].at[pl.ds(pl.multiple_of(own * rows, 16), rows), :], own_sem.at[k]
        )

    def to_mate(k):
        rows, _ = shapes[k]
        return send(
            ins[k], outs[k].at[pl.ds(pl.multiple_of(own * rows, 16), rows), :],
            q_send.at[k], q_recv.at[k], rep, mate,
        )

    def z_step(k, s, sign):
        w = window(k, s, rep)
        return send(w, w, z_send.at[k, s], z_recv.at[k, s], rep, own - 2 * sign)

    def x_step(k, s):
        w = window(k, s, rep)
        return send(w, w, x_send.at[k, s], x_recv.at[k, s], x_peer, own)

    def y_step(k, s):
        w = window(k, s, rep)
        return send(w, w, y_send.at[k, s], y_recv.at[k, s], y_peer, own)

    def d_by_y(k, s):
        w = window(k, s, x_peer)
        return send(w, w, d_send.at[k, s], d_recv.at[k, s], y_peer, own)

    def d_by_x(k, s):
        w = window(k, s, y_peer)
        return send(w, w, d_send.at[k, s], d_recv.at[k, s], x_peer, own)

    def p_step(k, s):
        w = window(k, s, None)
        return send(w, w, p_send.at[k, s], p_recv.at[k, s], rep, mate)

    items = [(k, h, sign) for k in range(count) for h in range(1, length) for sign in (1, -1)]

    def each(item, body):
        k, h, sign = item
        s = line + sign * h
        if sign > 0:
            there, further = s < length, line > 0
        else:
            there, further = s >= 0, line < length - 1

        @pl.when(there)
        def _():
            body(k, s, sign, further)

    def stage_z(k, s, sign, further):
        z_step(k, s, sign).wait_recv()

        @pl.when(further)
        def _():
            z_step(k, s, sign).start()

        x_step(k, s).start()
        y_step(k, s).start()

    def stage_xy(k, s, sign, further):
        x_step(k, s).wait_recv()
        y_step(k, s).wait_recv()

        @pl.when(s % 2 == 0)
        def _():
            d_by_y(k, s).start()

        @pl.when(s % 2 == 1)
        def _():
            d_by_x(k, s).start()

    def stage_d(k, s, sign, further):
        d_by_x(k, s).wait_recv()
        p_step(k, s).start()

    def stage_end(k, s, sign, further):
        @pl.when(further)
        def _():
            z_step(k, s, sign).wait_send()

        x_step(k, s).wait_send()
        y_step(k, s).wait_send()
        d_by_x(k, s).wait_send()
        p_step(k, s).wait_send()
        p_step(k, s).wait_recv()

    start_own(0)
    if count > 1:
        start_own(1)
    for k in range(count):
        local(k).start()
        to_mate(k).start()
    lag, total = 2, len(items)
    for i in range(total + 2 * lag):
        if i < total:
            k, h, sign = items[i]
            if h == 1 and sign == 1 and k >= 1 and k + 1 < count:
                start_own(k + 1)
            each(items[i], stage_z)
        if 0 <= i - lag < total:
            each(items[i - lag], stage_xy)
        if 0 <= i - 2 * lag < total:
            each(items[i - 2 * lag], stage_d)
    for item in items:
        each(item, stage_end)
    for k in range(count):
        local(k).wait()
        to_mate(k).wait()

        @pl.when(line > 0)
        def _():
            left(k).wait_send()

        @pl.when(line < length - 1)
        def _():
            right(k).wait_send()


def gather_all(shards, length, ident):
    shapes = tuple(s.shape for s in shards)
    count = len(shapes)
    sem = pltpu.SemaphoreType.DMA
    return pl.pallas_call(
        functools.partial(gather_kernel, shapes, length),
        out_shape=tuple(
            jax.ShapeDtypeStruct((2 * length * rows, cols), jnp.bfloat16) for rows, cols in shapes
        ),
        in_specs=[pl.BlockSpec(memory_space=pltpu.VMEM)] * count,
        out_specs=tuple(pl.BlockSpec(memory_space=pl.ANY) for _ in shapes),
        scratch_shapes=[sem((count,)), sem((count,)), sem((count,)), sem((count, 2))]
        + [sem((count, length))] * 10,
        compiler_params=pltpu.CompilerParams(collective_id=ident, has_side_effects=True),
        name="gather_all",
    )(*shards)


def reduce_kernel(shapes, length, *refs):
    count = len(shapes)
    ins, outs, rest = (refs[:count], refs[count : 2 * count], refs[2 * count :])
    held, other, first, second, third, fourth = (
        rest[count * j : count * (j + 1)] for j in range(6)
    )
    rest = rest[6 * count :]
    (l_sem, p_send, p_recv, a_send, a_recv, b_send, b_recv, z_send, z_recv) = rest[:9]
    (w_recv, e_sem, f_send, f_recv, g_send, g_recv, h_send, h_recv) = rest[9:]
    rep, own, line, core = places()
    x_bit, y_bit = rep % 2, rep // 2
    x_peer, y_peer = (rep + 1 - 2 * x_bit, (rep + 2) % 4)
    mate = own + 1 - 2 * core
    greet(rep, own, line, length)

    def send(src, dst, s_sem, r_sem, r, f):
        return pltpu.make_async_remote_copy(
            src_ref=src, dst_ref=dst, send_sem=s_sem, recv_sem=r_sem,
            device_id=dev(r, f), device_id_type=MESH_ID,
        )

    def bits(t):
        if t % 2 == 0:
            return x_bit, y_bit, x_peer, y_peer
        return y_bit, x_bit, y_peer, x_peer

    def block(k, t, side):
        rows, _ = shapes[k]
        return ins[k].at[pl.ds(pl.multiple_of((2 * t + side) * rows, 16), rows), :]

    def load(k, t):
        return pltpu.make_async_copy(block(k, t, core), held[k].at[t], l_sem.at[k, t])

    def p_step(k, t):
        return send(
            block(k, t, 1 - core), other[k].at[t], p_send.at[k, t], p_recv.at[k, t], rep, mate
        )

    def cut(index, width):
        return pl.ds(pl.multiple_of(index * width, 128), width)

    def a_step(k, t):
        a, _, peer, _ = bits(t)
        half = shapes[k][1] // 2
        return send(
            held[k].at[t, :, cut(1 - a, half)], first[k].at[t],
            a_send.at[k, t], a_recv.at[k, t], peer, own,
        )

    def b_step(k, t):
        _, b, _, peer = bits(t)
        quarter = shapes[k][1] // 4
        return send(
            first[k].at[t, :, cut(1 - b, quarter)], second[k].at[t],
            b_send.at[k, t], b_recv.at[k, t], peer, own,
        )

    def z_right(k, t):
        if t == length:
            return None
        return send(second[k].at[t], third[k].at[t], z_send.at[k, t], z_recv.at[k, t], rep, own + 2)

    def z_left(k, t, last):
        dst, sem = (fourth[k], w_recv.at[k]) if last else (third[k].at[t], z_recv.at[k, t])
        return send(second[k].at[t], dst, z_send.at[k, t], sem, rep, own - 2)

    def add(k, rows, body):
        step = 16 if rows % 32 else 32

        @pl.loop(0, rows, step=step)
        def _(r):
            body(pl.ds(pl.multiple_of(r, 16), step))

    def stage_a(k, t):
        load(k, t).wait()
        p_step(k, t).wait_recv()

        def body(r):
            held[k][t, r, :] = held[k][t, r, :] + other[k][t, r, :]

        add(k, shapes[k][0], body)
        a_step(k, t).start()

    def stage_b(k, t):
        a, _, _, _ = bits(t)
        half = shapes[k][1] // 2
        a_step(k, t).wait_recv()

        def body(r):
            first[k][t, r, :] = first[k][t, r, :] + held[k][t, r, cut(a, half)]

        add(k, shapes[k][0], body)
        b_step(k, t).start()

    def stage_c(k, t):
        _, b, _, _ = bits(t)
        quarter = shapes[k][1] // 4
        b_step(k, t).wait_recv()

        def body(r):
            second[k][t, r, :] = second[k][t, r, :] + first[k][t, r, cut(b, quarter)]

        add(k, shapes[k][0], body)

    def join(k, t, source):
        def body(r):
            second[k][t, r, :] = second[k][t, r, :] + source[r, :]

        add(k, shapes[k][0], body)

    def stage_z(k, t, hop):
        if hop < t:

            @pl.when(line == hop)
            def _():
                if hop > 0:
                    z_right(k, t).wait_recv()
                    join(k, t, third[k].at[t])
                z_right(k, t).start()

        place = length - 1 - hop
        if place > t:

            @pl.when(line == place)
            def _():
                if hop > 0:
                    z_left(k, t, False).wait_recv()
                    join(k, t, third[k].at[t])
                z_left(k, t, place - 1 == t).start()

    def piece(k, t, flip_a, flip_b):
        a, b, _, _ = bits(t)
        a = 1 - a if flip_a else a
        b = 1 - b if flip_b else b
        return outs[k].at[:, cut(2 * a + b, shapes[k][1] // 4)]

    def put(k, t):
        return pltpu.make_async_copy(second[k].at[t], piece(k, t, 0, 0), e_sem.at[k])

    def f_step(k, t):
        return send(
            second[k].at[t], piece(k, t, 0, 0), f_send.at[k], f_recv.at[k], bits(t)[2], own
        )

    def g_step(k, t):
        return send(
            second[k].at[t], piece(k, t, 0, 0), g_send.at[k], g_recv.at[k], bits(t)[3], own
        )

    def h_first(k, t):
        w = piece(k, t, 0, 1)
        return send(w, w, h_send.at[k], h_recv.at[k], bits(t)[2], own)

    def h_second(k, t):
        w = piece(k, t, 1, 0)
        return send(w, w, h_send.at[k], h_recv.at[k], bits(t)[3], own)

    def stage_e(k, t):
        @pl.when(line == t)
        def _():
            if t > 0:
                z_right(k, t).wait_recv()
                join(k, t, third[k].at[t])
            if t < length - 1:
                z_left(k, t, True).wait_recv()
                join(k, t, fourth[k])
            put(k, t).start()
            f_step(k, t).start()
            g_step(k, t).start()

    def stage_f(k, t):
        @pl.when(line == t)
        def _():
            f_step(k, t).wait_recv()
            g_step(k, t).wait_recv()

            @pl.when(core == 0)
            def _():
                h_first(k, t).start()

            @pl.when(core == 1)
            def _():
                h_second(k, t).start()

    items = [(k, t) for k in range(count) for t in range(length)]
    for item in items:
        load(*item).start()
        p_step(*item).start()
    total, lag = len(items), 2
    plan = [(0, stage_a), (lag, stage_b), (2 * lag, stage_c)]
    for hop in range(length - 1):
        plan.append((3 * lag - 2 + hop * lag, functools.partial(stage_z, hop=hop)))
    plan.append((3 * lag - 2 + (length - 1) * lag, stage_e))
    plan.append((3 * lag - 2 + (length + 1) * lag, stage_f))
    for i in range(total + plan[-1][0]):
        for late, stage in plan:
            if 0 <= i - late < total:
                stage(*items[i - late])
    for k, t in items:
        p_step(k, t).wait_send()
        a_step(k, t).wait_send()
        b_step(k, t).wait_send()

        @pl.when(line < t)
        def _():
            z_right(k, t).wait_send()

        @pl.when(line > t)
        def _():
            z_left(k, t, False).wait_send()

        @pl.when(line == t)
        def _():
            put(k, t).wait()
            f_step(k, t).wait_send()
            g_step(k, t).wait_send()
            h_first(k, t).wait_send()
            h_first(k, t).wait_recv()


def reduce_all(arrays, length, ident):
    shapes = tuple((a.shape[0] // (2 * length), a.shape[1]) for a in arrays)
    count = len(shapes)
    sem = pltpu.SemaphoreType.DMA

    def room(part, lead=True):
        return [
            pltpu.VMEM(((length,) if lead else ()) + (rows, cols // part), jnp.bfloat16)
            for rows, cols in shapes
        ]

    return pl.pallas_call(
        functools.partial(reduce_kernel, shapes, length),
        out_shape=tuple(jax.ShapeDtypeStruct(s, jnp.bfloat16) for s in shapes),
        in_specs=[pl.BlockSpec(memory_space=pl.ANY)] * count,
        out_specs=tuple(pl.BlockSpec(memory_space=pl.ANY) for _ in shapes),
        scratch_shapes=room(1) + room(1) + room(2) + room(4) + room(4) + room(4, False)
        + [sem((count, length))] * 9
        + [sem((count,))] * 8,
        compiler_params=pltpu.CompilerParams(
            collective_id=ident, has_side_effects=True, vmem_limit_bytes=64 * 1024 * 1024 - 65536
        ),
        name="reduce_all",
    )(*arrays)


def vectors_in(vectors):
    flat = jnp.concatenate(vectors)
    wide = 512 * -(-flat.shape[0] // 512)
    flat = jnp.pad(flat, (0, wide - flat.shape[0]))
    return jnp.broadcast_to(flat[None, :], (16, wide))


def vectors_out(packed, sizes):
    table = packed.reshape(packed.shape[0] // 16, 16, packed.shape[1])[:, 0]
    results, offset = [], 0
    for size in sizes:
        results.append(table[:, offset : offset + size].reshape(-1))
        offset += size
    return results


def gather_plain(shards_of):
    return [lax.all_gather(shard, "fsdp", axis=0, tiled=True) for shard in shards_of]


def reduce_plain(arrays):
    return [
        lax.psum(lax.psum_scatter(array, "fsdp", scatter_dimension=0, tiled=True), "rep")
        for array in arrays
    ]


def shards(
    extents,
    patches,
    enc_gain1,
    enc_qkv,
    enc_proj,
    enc_gain2,
    enc_up,
    enc_down,
    embed_w,
    mask_token,
    dec_gain1,
    dec_qkv,
    dec_proj,
    dec_gain2,
    dec_up,
    dec_down,
    visible,
    unshuffle,
    ground_dist,
    cotangent,
):
    images, slot_count, model_width = patches.shape
    patch_count = unshuffle.shape[1]
    dec_width = embed_w.shape[1]
    members = extents["fsdp"]
    direct = members == 8 and extents["rep"] == 4

    vectors = (enc_gain1, enc_gain2, mask_token, dec_gain1, dec_gain2)
    sizes = [v.shape[0] for v in vectors]
    weights = (
        vectors_in(vectors),
        enc_qkv,
        enc_proj,
        enc_up,
        enc_down,
        embed_w,
        dec_qkv,
        dec_proj,
        dec_up,
        dec_down,
    )
    if direct:
        whole = gather_all(weights, members // 2, 0)
    else:
        whole = gather_plain(weights)
    full_gain1, full_gain2, full_mask, full_dec1, full_dec2 = vectors_out(whole[0], sizes)
    enc_full = (full_gain1, whole[1], whole[2], full_gain2, whole[3], whole[4])
    dec_full = (full_dec1, whole[6], whole[7], full_dec2, whole[8], whole[9])
    full_embed = whole[5]

    rows_in = patches.astype(jnp.float32).reshape(images * slot_count, model_width)
    enc_rows, enc_state = block_forward(rows_in, enc_full, visible, HEADS, images, slot_count)
    enc_low = enc_rows.astype(jnp.bfloat16)
    embedded = matmul(enc_low, full_embed).reshape(images, slot_count, dec_width)
    picked = jnp.take_along_axis(
        embedded, jnp.minimum(unshuffle, slot_count - 1)[:, :, None], axis=1
    )
    shown_rows = (unshuffle < visible[:, None])[:, :, None]
    dec_in = jnp.where(
        shown_rows, picked, full_mask.astype(jnp.float32)[None, None, :]
    ) + position_table(ground_dist, GRID, dec_width)
    all_live = jnp.full((images,), patch_count, jnp.int32)
    dec_rows, dec_state = block_forward(
        dec_in.reshape(images * patch_count, dec_width),
        dec_full,
        all_live,
        HEADS_D,
        images,
        patch_count,
    )
    d_dec = cotangent.astype(jnp.float32).reshape(images * patch_count, dec_width)
    d_dec_in, dec_grads = block_backward(
        dec_state, d_dec, dec_full, all_live, HEADS_D, images, patch_count
    )
    d_positions = d_dec_in.reshape(images, patch_count, dec_width)
    grad_mask = jnp.sum(jnp.where(shown_rows, 0.0, d_positions), axis=(0, 1))
    inverse = jnp.argsort(unshuffle, axis=1)[:, :slot_count]
    slot_live = (jnp.arange(slot_count, dtype=jnp.int32)[None, :] < visible[:, None])[:, :, None]
    d_embed = jnp.where(
        slot_live, jnp.take_along_axis(d_positions, inverse[:, :, None], axis=1), 0.0
    )
    d_embed_low = d_embed.reshape(images * slot_count, dec_width).astype(jnp.bfloat16)
    grad_embed = matmul_tn(enc_low, d_embed_low)
    d_enc = matmul_nt(d_embed_low, full_embed)
    d_rows_in, enc_grads = block_backward(
        enc_state, d_enc, enc_full, visible, HEADS, images, slot_count
    )

    vector_grads = (enc_grads[0], enc_grads[3], grad_mask, dec_grads[0], dec_grads[3])
    table = jnp.concatenate([g.reshape(members, -1) for g in vector_grads], axis=1)
    wide = 512 * -(-table.shape[1] // 512)
    table = jnp.pad(table, ((0, 0), (0, wide - table.shape[1])))
    table = jnp.broadcast_to(table[:, None, :], (members, 16, wide)).reshape(members * 16, wide)
    gradients = [
        item.astype(jnp.bfloat16)
        for item in (
            dec_grads[5],
            dec_grads[4],
            dec_grads[1],
            dec_grads[2],
            grad_embed,
            enc_grads[5],
            enc_grads[4],
            enc_grads[2],
            enc_grads[1],
            table,
        )
    ]
    if direct:
        sums = reduce_all(gradients, members // 2, 1)
    else:
        sums = reduce_plain(gradients)
    sums = [item.astype(jnp.float32) for item in sums]
    small = vectors_out(sums[9], sizes)
    return (
        enc_low.reshape(images, slot_count, model_width),
        dec_rows.astype(jnp.bfloat16).reshape(images, patch_count, dec_width),
        d_rows_in.astype(jnp.bfloat16).reshape(images, slot_count, model_width),
        small[0],
        sums[8],
        sums[7],
        small[1],
        sums[6],
        sums[5],
        sums[4],
        small[2],
        small[3],
        sums[2],
        sums[3],
        small[4],
        sums[1],
        sums[0],
    )


def solution(mesh):
    placed = (
        P(("rep", "fsdp"), None, None),
        P("fsdp"),
        P("fsdp", None),
        P("fsdp", None),
        P("fsdp"),
        P("fsdp", None),
        P("fsdp", None),
        P("fsdp", None),
        P("fsdp"),
        P("fsdp"),
        P("fsdp", None),
        P("fsdp", None),
        P("fsdp"),
        P("fsdp", None),
        P("fsdp", None),
        P(("rep", "fsdp")),
        P(("rep", "fsdp"), None),
        P(("rep", "fsdp")),
        P(("rep", "fsdp"), None, None),
    )
    return jax.shard_map(
        functools.partial(shards, dict(mesh.shape)),
        mesh=mesh,
        in_specs=placed,
        out_specs=(
            P(("rep", "fsdp"), None, None),
            P(("rep", "fsdp"), None, None),
            P(("rep", "fsdp"), None, None),
            P("fsdp"),
            P("fsdp", None),
            P("fsdp", None),
            P("fsdp"),
            P("fsdp", None),
            P("fsdp", None),
            P("fsdp", None),
            P("fsdp"),
            P("fsdp"),
            P("fsdp", None),
            P("fsdp", None),
            P("fsdp"),
            P("fsdp", None),
            P("fsdp", None),
        ),
        check_vma=False,
    )
```

```python
import functools
import math

import jax
import jax.numpy as jnp
from jax import lax
from jax.experimental import pallas as pl
from jax.experimental.pallas import tpu as pltpu
from jax.sharding import PartitionSpec as P

HEADS = 16
HEADS_D = 16
GRID = 16


norm_epsilon = 1e-06


def matmul(left, right):
    return jnp.dot(left, right, preferred_element_type=jnp.float32)


def matmul_tn(left, right):
    return lax.dot_general(
        left, right, (((0,), (0,)), ((), ())), preferred_element_type=jnp.float32
    )


def matmul_nt(left, right):
    return lax.dot_general(
        left, right, (((1,), (1,)), ((), ())), preferred_element_type=jnp.float32
    )


def norm_stats(values):
    centre = values - jnp.mean(values, axis=-1, keepdims=True)
    inv_dev = lax.rsqrt(jnp.mean(centre * centre, axis=-1, keepdims=True) + norm_epsilon)
    return (centre * inv_dev, inv_dev)


def norm_back(d_scaled, normal, inv_dev):
    return inv_dev * (
        d_scaled
        - jnp.mean(d_scaled, axis=-1, keepdims=True)
        - normal * jnp.mean(d_scaled * normal, axis=-1, keepdims=True)
    )


def position_table(distance, grid_side, model_width):
    quarter = model_width // 4
    frequency = 1.0 / 10000.0 ** (jnp.arange(quarter, dtype=jnp.float32) / quarter)
    places = jnp.arange(grid_side * grid_side, dtype=jnp.int32)
    column = (places % grid_side).astype(jnp.float32)
    row_pos = (places // grid_side).astype(jnp.float32)
    along_c = distance[:, None, None] * column[None, :, None] * frequency[None, None, :]
    along_r = distance[:, None, None] * row_pos[None, :, None] * frequency[None, None, :]
    return jnp.concatenate(
        [jnp.sin(along_c), jnp.cos(along_c), jnp.sin(along_r), jnp.cos(along_r)], axis=-1
    )


def by_groups(function, members, length):
    images = members[0].shape[0]
    per_step = math.gcd(images, max(1, 512 // length))
    shaped = tuple(
        (member.reshape((images // per_step, per_step) + member.shape[1:]) for member in members)
    )
    results = lax.map(lambda group_items: function(*group_items), shaped)
    return jax.tree.map(lambda result: result.reshape((images,) + result.shape[2:]), results)


def masked_scores(queries, key_rows, live, score_scale):
    raw_scores = (
        jnp.einsum("nqhd,nkhd->nhqk", queries, key_rows, preferred_element_type=jnp.float32)
        * score_scale
    )
    length = key_rows.shape[1]
    valid = jnp.arange(length, dtype=jnp.int32)[None, None, None, :] < live[:, None, None, None]
    return jnp.where(valid, raw_scores, -1e30)


def split_heads(packed, head_count):
    images, length, three_width = packed.shape
    split_parts = packed.reshape(images, length, 3, head_count, three_width // (3 * head_count))
    return (split_parts[:, :, 0], split_parts[:, :, 1], split_parts[:, :, 2])


def attend_group(packed, live, head_count, score_scale):
    queries, key_rows, value_rows = split_heads(packed, head_count)
    scores = masked_scores(queries, key_rows, live, score_scale)
    highest = jnp.max(scores, axis=-1, keepdims=True)
    exponent = jnp.exp(scores - highest)
    summed = jnp.sum(exponent, axis=-1, keepdims=True)
    soft_weights = (exponent / summed).astype(jnp.bfloat16)
    mixed_rows = jnp.einsum(
        "nhqk,nkhd->nqhd", soft_weights, value_rows, preferred_element_type=jnp.float32
    )
    images, length = (packed.shape[0], packed.shape[1])
    log_total = (highest + jnp.log(summed))[..., 0]
    return (
        mixed_rows.reshape(images, length, packed.shape[2] // 3).astype(jnp.bfloat16),
        log_total,
    )


def attend_back_group(packed, log_total, d_mixed, live, head_count, score_scale):
    queries, key_rows, value_rows = split_heads(packed, head_count)
    scores = masked_scores(queries, key_rows, live, score_scale)
    soft_float = jnp.exp(scores - log_total[..., None])
    d_heads = d_mixed.reshape(queries.shape)
    d_soft = jnp.einsum("nqhd,nkhd->nhqk", d_heads, value_rows, preferred_element_type=jnp.float32)
    row_dot = jnp.sum(soft_float * d_soft, axis=-1, keepdims=True)
    d_scores = (soft_float * (d_soft - row_dot)).astype(jnp.bfloat16)
    d_queries = (
        jnp.einsum("nhqk,nkhd->nqhd", d_scores, key_rows, preferred_element_type=jnp.float32)
        * score_scale
    )
    d_keys = (
        jnp.einsum("nhqk,nqhd->nkhd", d_scores, queries, preferred_element_type=jnp.float32)
        * score_scale
    )
    d_values = jnp.einsum(
        "nhqk,nqhd->nkhd",
        soft_float.astype(jnp.bfloat16),
        d_heads,
        preferred_element_type=jnp.float32,
    )
    stacked = jnp.stack([d_queries, d_keys, d_values], axis=2)
    return stacked.reshape(packed.shape).astype(jnp.bfloat16)


def block_forward(rows, weights, live, head_count, images, length):
    gain_one, w_qkv, w_out, gain_two, w_up, w_down = weights
    model_width = rows.shape[-1]
    score_scale = (model_width // head_count) ** (-0.5)
    normal_one, inv_one = norm_stats(rows)
    normed_one = (normal_one * gain_one).astype(jnp.bfloat16)
    packed = matmul(normed_one, w_qkv).astype(jnp.bfloat16).reshape(images, length, 3 * model_width)

    def attend(group_packed, group_live):
        return attend_group(group_packed, group_live, head_count, score_scale)

    mixed_rows, log_total = by_groups(attend, (packed, live), length)
    middle = rows + matmul(mixed_rows.reshape(images * length, model_width), w_out)
    normal_two, inv_two = norm_stats(middle)
    normed_two = (normal_two * gain_two).astype(jnp.bfloat16)
    hidden = jax.nn.gelu(matmul(normed_two, w_up), approximate=False).astype(jnp.bfloat16)
    return (middle + matmul(hidden, w_down), (rows, packed, mixed_rows, log_total, middle))


def block_backward(kept_state, d_out, weights, live, head_count, images, length):
    rows, packed, mixed_rows, log_total, middle = kept_state
    gain_one, w_qkv, w_out, gain_two, w_up, w_down = weights
    model_width = rows.shape[-1]
    score_scale = (model_width // head_count) ** (-0.5)
    normal_two, inv_two = norm_stats(middle)
    normed_two = (normal_two * gain_two).astype(jnp.bfloat16)
    up_proj = matmul(normed_two, w_up)
    hidden_float, gelu_back = jax.vjp(lambda inner: jax.nn.gelu(inner, approximate=False), up_proj)
    hidden = hidden_float.astype(jnp.bfloat16)
    d_branch = d_out.astype(jnp.bfloat16)
    grad_down = matmul_tn(hidden, d_branch)
    d_hidden = matmul_nt(d_branch, w_down)
    d_up = gelu_back(d_hidden)[0].astype(jnp.bfloat16)
    grad_up = matmul_tn(normed_two, d_up)
    d_normed_two = matmul_nt(d_up, w_up)
    grad_gain_two = jnp.sum(d_normed_two * normal_two, axis=0)
    d_middle = d_out + norm_back(d_normed_two * gain_two, normal_two, inv_two)
    d_attn = d_middle.astype(jnp.bfloat16)
    grad_out = matmul_tn(mixed_rows.reshape(images * length, model_width), d_attn)
    d_mixed = matmul_nt(d_attn, w_out).astype(jnp.bfloat16).reshape(images, length, model_width)

    def attend_back(group_packed, group_total, group_grad, group_live):
        return attend_back_group(
            group_packed, group_total, group_grad, group_live, head_count, score_scale
        )

    d_packed = by_groups(attend_back, (packed, log_total, d_mixed, live), length)
    d_packed = d_packed.reshape(images * length, 3 * model_width)
    normal_one, inv_one = norm_stats(rows)
    normed_one = (normal_one * gain_one).astype(jnp.bfloat16)
    grad_qkv = matmul_tn(normed_one, d_packed)
    d_normed_one = matmul_nt(d_packed, w_qkv)
    grad_gain_one = jnp.sum(d_normed_one * normal_one, axis=0)
    d_rows = d_middle + norm_back(d_normed_one * gain_one, normal_one, inv_one)
    return (d_rows, (grad_gain_one, grad_qkv, grad_out, grad_gain_two, grad_up, grad_down))


MESH_ID = pl.DeviceIdType.MESH


def places():
    rep = lax.axis_index("rep")
    own = lax.axis_index("fsdp")
    return rep, own, own // 2, own % 2


def dev(rep, own):
    return {"rep": rep, "fsdp": own}


def greet(rep, own, line, length):
    barrier = pltpu.get_barrier_semaphore()

    def call(r, f):
        pl.semaphore_signal(barrier, inc=1, device_id=dev(r, f), device_id_type=MESH_ID)

    call(rep, own + 1 - 2 * (own % 2))
    call(rep + 1 - 2 * (rep % 2), own)
    call((rep + 2) % 4, own)

    @pl.when(line > 0)
    def _():
        call(rep, own - 2)

    @pl.when(line < length - 1)
    def _():
        call(rep, own + 2)

    ends = (line == 0).astype(jnp.int32) + (line == length - 1).astype(jnp.int32)
    pl.semaphore_wait(barrier, 5 - ends)


def gather_kernel(shapes, length, *refs):
    count = len(shapes)
    ins, outs, rest = (refs[:count], refs[count : 2 * count], refs[2 * count :])
    (own_sem, q_send, q_recv, o_send, z_send, z_recv, x_send, x_recv, y_send, y_recv) = rest[:10]
    d_send, d_recv, p_send, p_recv = rest[10:]
    rep, own, line, core = places()
    x_peer, y_peer = (rep + 1 - 2 * (rep % 2), (rep + 2) % 4)
    mate = own + 1 - 2 * core
    greet(rep, own, line, length)

    def window(k, source, quarter):
        rows, cols = shapes[k]
        start = pl.multiple_of((2 * source + core) * rows, 16)
        if quarter is None:
            return outs[k].at[pl.ds(start, rows), :]
        return outs[k].at[
            pl.ds(start, rows), pl.ds(pl.multiple_of(quarter * (cols // 4), 128), cols // 4)
        ]

    def send(src, dst, s_sem, r_sem, r, f):
        return pltpu.make_async_remote_copy(
            src_ref=src, dst_ref=dst, send_sem=s_sem, recv_sem=r_sem,
            device_id=dev(r, f), device_id_type=MESH_ID,
        )

    def mine(k):
        _, cols = shapes[k]
        return ins[k].at[:, pl.ds(pl.multiple_of(rep * (cols // 4), 128), cols // 4)]

    def left(k):
        return send(mine(k), window(k, line, rep), o_send.at[k, 0], z_recv.at[k, line], rep, own - 2)

    def right(k):
        return send(mine(k), window(k, line, rep), o_send.at[k, 1], z_recv.at[k, line], rep, own + 2)

    def start_own(k):
        @pl.when(line > 0)
        def _():
            left(k).start()

        @pl.when(line < length - 1)
        def _():
            right(k).start()

    def local(k):
        rows, _ = shapes[k]
        return pltpu.make_async_copy(
            ins[k], outs[k].at[pl.ds(pl.multiple_of(own * rows, 16), rows), :], own_sem.at[k]
        )

    def to_mate(k):
        rows, _ = shapes[k]
        return send(
            ins[k], outs[k].at[pl.ds(pl.multiple_of(own * rows, 16), rows), :],
            q_send.at[k], q_recv.at[k], rep, mate,
        )

    def z_step(k, s, sign):
        w = window(k, s, rep)
        return send(w, w, z_send.at[k, s], z_recv.at[k, s], rep, own - 2 * sign)

    def x_step(k, s):
        w = window(k, s, rep)
        return send(w, w, x_send.at[k, s], x_recv.at[k, s], x_peer, own)

    def y_step(k, s):
        w = window(k, s, rep)
        return send(w, w, y_send.at[k, s], y_recv.at[k, s], y_peer, own)

    def d_by_y(k, s):
        w = window(k, s, x_peer)
        return send(w, w, d_send.at[k, s], d_recv.at[k, s], y_peer, own)

    def d_by_x(k, s):
        w = window(k, s, y_peer)
        return send(w, w, d_send.at[k, s], d_recv.at[k, s], x_peer, own)

    def p_step(k, s):
        w = window(k, s, None)
        return send(w, w, p_send.at[k, s], p_recv.at[k, s], rep, mate)

    items = [(k, h, sign) for k in range(count) for h in range(1, length) for sign in (1, -1)]

    def each(item, body):
        k, h, sign = item
        s = line + sign * h
        if sign > 0:
            there, further = s < length, line > 0
        else:
            there, further = s >= 0, line < length - 1

        @pl.when(there)
        def _():
            body(k, s, sign, further)

    def stage_z(k, s, sign, further):
        z_step(k, s, sign).wait_recv()

        @pl.when(further)
        def _():
            z_step(k, s, sign).start()

        x_step(k, s).start()
        y_step(k, s).start()

    def stage_xy(k, s, sign, further):
        x_step(k, s).wait_recv()
        y_step(k, s).wait_recv()

        @pl.when((s + core) % 2 == 0)
        def _():
            d_by_y(k, s).start()

        @pl.when((s + core) % 2 == 1)
        def _():
            d_by_x(k, s).start()

    def stage_d(k, s, sign, further):
        d_by_x(k, s).wait_recv()
        p_step(k, s).start()

    def stage_end(k, s, sign, further):
        @pl.when(further)
        def _():
            z_step(k, s, sign).wait_send()

        x_step(k, s).wait_send()
        y_step(k, s).wait_send()
        d_by_x(k, s).wait_send()
        p_step(k, s).wait_send()
        p_step(k, s).wait_recv()

    start_own(0)
    if count > 1:
        start_own(1)
    for k in range(count):
        local(k).start()
        to_mate(k).start()
    lag, total = 6, len(items)
    for i in range(total + 2 * lag):
        if i < total:
            k, h, sign = items[i]
            if h == 1 and sign == 1 and k >= 1 and k + 1 < count:
                start_own(k + 1)
            each(items[i], stage_z)
        if 0 <= i - lag < total:
            each(items[i - lag], stage_xy)
        if 0 <= i - 2 * lag < total:
            each(items[i - 2 * lag], stage_d)
    for item in items:
        each(item, stage_end)
    for k in range(count):
        local(k).wait()
        to_mate(k).wait()

        @pl.when(line > 0)
        def _():
            left(k).wait_send()

        @pl.when(line < length - 1)
        def _():
            right(k).wait_send()


def gather_all(shards, length, ident):
    shapes = tuple(s.shape for s in shards)
    count = len(shapes)
    sem = pltpu.SemaphoreType.DMA
    return pl.pallas_call(
        functools.partial(gather_kernel, shapes, length),
        out_shape=tuple(
            jax.ShapeDtypeStruct((2 * length * rows, cols), jnp.bfloat16) for rows, cols in shapes
        ),
        in_specs=[pl.BlockSpec(memory_space=pltpu.VMEM)] * count,
        out_specs=tuple(pl.BlockSpec(memory_space=pl.ANY) for _ in shapes),
        scratch_shapes=[sem((count,)), sem((count,)), sem((count,)), sem((count, 2))]
        + [sem((count, length))] * 10,
        compiler_params=pltpu.CompilerParams(collective_id=ident, has_side_effects=True),
        name="gather_all",
    )(*shards)


def reduce_kernel(shapes, length, *refs):
    count = len(shapes)
    ins, outs, rest = (refs[:count], refs[count : 2 * count], refs[2 * count :])
    held, other, first, second, third, fourth = (
        rest[count * j : count * (j + 1)] for j in range(6)
    )
    rest = rest[6 * count :]
    (l_sem, p_send, p_recv, a_send, a_recv, b_send, b_recv, z_send, z_recv) = rest[:9]
    (w_recv, e_sem, f_send, f_recv, g_send, g_recv, h_send, h_recv) = rest[9:]
    rep, own, line, core = places()
    x_bit, y_bit = rep % 2, rep // 2
    x_peer, y_peer = (rep + 1 - 2 * x_bit, (rep + 2) % 4)
    mate = own + 1 - 2 * core
    greet(rep, own, line, length)

    def send(src, dst, s_sem, r_sem, r, f):
        return pltpu.make_async_remote_copy(
            src_ref=src, dst_ref=dst, send_sem=s_sem, recv_sem=r_sem,
            device_id=dev(r, f), device_id_type=MESH_ID,
        )

    def bits(t):
        if t % 2 == 0:
            return x_bit, y_bit, x_peer, y_peer
        return y_bit, x_bit, y_peer, x_peer

    def block(k, t, side):
        rows, _ = shapes[k]
        return ins[k].at[pl.ds(pl.multiple_of((2 * t + side) * rows, 16), rows), :]

    def load(k, t):
        return pltpu.make_async_copy(block(k, t, core), held[k].at[t], l_sem.at[k, t])

    def p_step(k, t):
        return send(
            block(k, t, 1 - core), other[k].at[t], p_send.at[k, t], p_recv.at[k, t], rep, mate
        )

    def cut(index, width):
        return pl.ds(pl.multiple_of(index * width, 128), width)

    def a_step(k, t):
        a, _, peer, _ = bits(t)
        half = shapes[k][1] // 2
        return send(
            held[k].at[t, :, cut(1 - a, half)], first[k].at[t],
            a_send.at[k, t], a_recv.at[k, t], peer, own,
        )

    def b_step(k, t):
        _, b, _, peer = bits(t)
        quarter = shapes[k][1] // 4
        return send(
            first[k].at[t, :, cut(1 - b, quarter)], second[k].at[t],
            b_send.at[k, t], b_recv.at[k, t], peer, own,
        )

    def z_right(k, t):
        if t == length:
            return None
        return send(second[k].at[t], third[k].at[t], z_send.at[k, t], z_recv.at[k, t], rep, own + 2)

    def z_left(k, t, last):
        dst, sem = (fourth[k], w_recv.at[k]) if last else (third[k].at[t], z_recv.at[k, t])
        return send(second[k].at[t], dst, z_send.at[k, t], sem, rep, own - 2)

    def add(k, rows, body):
        step = 16 if rows % 32 else 32

        @pl.loop(0, rows, step=step)
        def _(r):
            body(pl.ds(pl.multiple_of(r, 16), step))

    def stage_a(k, t):
        load(k, t).wait()
        p_step(k, t).wait_recv()

        def body(r):
            held[k][t, r, :] = held[k][t, r, :] + other[k][t, r, :]

        add(k, shapes[k][0], body)
        a_step(k, t).start()

    def stage_b(k, t):
        a, _, _, _ = bits(t)
        half = shapes[k][1] // 2
        a_step(k, t).wait_recv()

        def body(r):
            first[k][t, r, :] = first[k][t, r, :] + held[k][t, r, cut(a, half)]

        add(k, shapes[k][0], body)
        b_step(k, t).start()

    def stage_c(k, t):
        _, b, _, _ = bits(t)
        quarter = shapes[k][1] // 4
        b_step(k, t).wait_recv()

        def body(r):
            second[k][t, r, :] = second[k][t, r, :] + first[k][t, r, cut(b, quarter)]

        add(k, shapes[k][0], body)

    def join(k, t, source):
        def body(r):
            second[k][t, r, :] = second[k][t, r, :] + source[r, :]

        add(k, shapes[k][0], body)

    def stage_z(k, t, hop):
        if hop < t:

            @pl.when(line == hop)
            def _():
                if hop > 0:
                    z_right(k, t).wait_recv()
                    join(k, t, third[k].at[t])
                z_right(k, t).start()

        place = length - 1 - hop
        if place > t:

            @pl.when(line == place)
            def _():
                if hop > 0:
                    z_left(k, t, False).wait_recv()
                    join(k, t, third[k].at[t])
                z_left(k, t, place - 1 == t).start()

    def piece(k, t, flip_a, flip_b):
        a, b, _, _ = bits(t)
        a = 1 - a if flip_a else a
        b = 1 - b if flip_b else b
        return outs[k].at[:, cut(2 * a + b, shapes[k][1] // 4)]

    def put(k, t):
        return pltpu.make_async_copy(second[k].at[t], piece(k, t, 0, 0), e_sem.at[k])

    def f_step(k, t):
        return send(
            second[k].at[t], piece(k, t, 0, 0), f_send.at[k], f_recv.at[k], bits(t)[2], own
        )

    def g_step(k, t):
        return send(
            second[k].at[t], piece(k, t, 0, 0), g_send.at[k], g_recv.at[k], bits(t)[3], own
        )

    def h_first(k, t):
        w = piece(k, t, 0, 1)
        return send(w, w, h_send.at[k], h_recv.at[k], bits(t)[2], own)

    def h_second(k, t):
        w = piece(k, t, 1, 0)
        return send(w, w, h_send.at[k], h_recv.at[k], bits(t)[3], own)

    def stage_e(k, t):
        @pl.when(line == t)
        def _():
            if t > 0:
                z_right(k, t).wait_recv()
                join(k, t, third[k].at[t])
            if t < length - 1:
                z_left(k, t, True).wait_recv()
                join(k, t, fourth[k])
            put(k, t).start()
            f_step(k, t).start()
            g_step(k, t).start()

    def stage_f(k, t):
        @pl.when(line == t)
        def _():
            f_step(k, t).wait_recv()
            g_step(k, t).wait_recv()

            @pl.when(core == 0)
            def _():
                h_first(k, t).start()

            @pl.when(core == 1)
            def _():
                h_second(k, t).start()

    items = [(k, t) for k in range(count) for t in range(length)]
    for item in items:
        load(*item).start()
        p_step(*item).start()
    total, lag = len(items), 4
    plan = [(0, stage_a), (lag, stage_b), (2 * lag, stage_c)]
    for hop in range(length - 1):
        plan.append((3 * lag - 2 + hop * lag, functools.partial(stage_z, hop=hop)))
    plan.append((3 * lag - 2 + (length - 1) * lag, stage_e))
    plan.append((3 * lag - 2 + (length + 1) * lag, stage_f))
    for i in range(total + plan[-1][0]):
        for late, stage in plan:
            if 0 <= i - late < total:
                stage(*items[i - late])
    for k, t in items:
        p_step(k, t).wait_send()
        a_step(k, t).wait_send()
        b_step(k, t).wait_send()

        @pl.when(line < t)
        def _():
            z_right(k, t).wait_send()

        @pl.when(line > t)
        def _():
            z_left(k, t, False).wait_send()

        @pl.when(line == t)
        def _():
            put(k, t).wait()
            f_step(k, t).wait_send()
            g_step(k, t).wait_send()
            h_first(k, t).wait_send()
            h_first(k, t).wait_recv()


def reduce_all(arrays, length, ident):
    shapes = tuple((a.shape[0] // (2 * length), a.shape[1]) for a in arrays)
    count = len(shapes)
    sem = pltpu.SemaphoreType.DMA

    def room(part, lead=True):
        return [
            pltpu.VMEM(((length,) if lead else ()) + (rows, cols // part), jnp.bfloat16)
            for rows, cols in shapes
        ]

    return pl.pallas_call(
        functools.partial(reduce_kernel, shapes, length),
        out_shape=tuple(jax.ShapeDtypeStruct(s, jnp.bfloat16) for s in shapes),
        in_specs=[pl.BlockSpec(memory_space=pl.ANY)] * count,
        out_specs=tuple(pl.BlockSpec(memory_space=pl.ANY) for _ in shapes),
        scratch_shapes=room(1) + room(1) + room(2) + room(4) + room(4) + room(4, False)
        + [sem((count, length))] * 9
        + [sem((count,))] * 8,
        compiler_params=pltpu.CompilerParams(
            collective_id=ident, has_side_effects=True, vmem_limit_bytes=64 * 1024 * 1024 - 65536
        ),
        name="reduce_all",
    )(*arrays)


def vectors_in(vectors):
    flat = jnp.concatenate(vectors)
    wide = 512 * -(-flat.shape[0] // 512)
    flat = jnp.pad(flat, (0, wide - flat.shape[0]))
    return jnp.broadcast_to(flat[None, :], (16, wide))


def vectors_out(packed, sizes):
    table = packed.reshape(packed.shape[0] // 16, 16, packed.shape[1])[:, 0]
    results, offset = [], 0
    for size in sizes:
        results.append(table[:, offset : offset + size].reshape(-1))
        offset += size
    return results


def gather_plain(shards_of):
    return [lax.all_gather(shard, "fsdp", axis=0, tiled=True) for shard in shards_of]


def reduce_plain(arrays):
    return [
        lax.psum(lax.psum_scatter(array, "fsdp", scatter_dimension=0, tiled=True), "rep")
        for array in arrays
    ]


def shards(
    extents,
    patches,
    enc_gain1,
    enc_qkv,
    enc_proj,
    enc_gain2,
    enc_up,
    enc_down,
    embed_w,
    mask_token,
    dec_gain1,
    dec_qkv,
    dec_proj,
    dec_gain2,
    dec_up,
    dec_down,
    visible,
    unshuffle,
    ground_dist,
    cotangent,
):
    images, slot_count, model_width = patches.shape
    patch_count = unshuffle.shape[1]
    dec_width = embed_w.shape[1]
    members = extents["fsdp"]
    direct = members == 8 and extents["rep"] == 4

    vectors = (enc_gain1, enc_gain2, mask_token, dec_gain1, dec_gain2)
    sizes = [v.shape[0] for v in vectors]
    front = (vectors_in(vectors), enc_qkv, enc_proj, enc_up)
    behind = (enc_down, embed_w, dec_qkv, dec_proj, dec_up, dec_down)
    later = gather_plain(behind)
    if direct:
        whole = gather_all(front, members // 2, 0)
    else:
        whole = gather_plain(front)
    full_gain1, full_gain2, full_mask, full_dec1, full_dec2 = vectors_out(whole[0], sizes)
    enc_full = (full_gain1, whole[1], whole[2], full_gain2, whole[3], later[0])
    dec_full = (full_dec1, later[2], later[3], full_dec2, later[4], later[5])
    full_embed = later[1]

    rows_in = patches.astype(jnp.float32).reshape(images * slot_count, model_width)
    enc_rows, enc_state = block_forward(rows_in, enc_full, visible, HEADS, images, slot_count)
    enc_low = enc_rows.astype(jnp.bfloat16)
    embedded = matmul(enc_low, full_embed).reshape(images, slot_count, dec_width)
    picked = jnp.take_along_axis(
        embedded, jnp.minimum(unshuffle, slot_count - 1)[:, :, None], axis=1
    )
    shown_rows = (unshuffle < visible[:, None])[:, :, None]
    dec_in = jnp.where(
        shown_rows, picked, full_mask.astype(jnp.float32)[None, None, :]
    ) + position_table(ground_dist, GRID, dec_width)
    all_live = jnp.full((images,), patch_count, jnp.int32)
    dec_rows, dec_state = block_forward(
        dec_in.reshape(images * patch_count, dec_width),
        dec_full,
        all_live,
        HEADS_D,
        images,
        patch_count,
    )
    d_dec = cotangent.astype(jnp.float32).reshape(images * patch_count, dec_width)
    d_dec_in, dec_grads = block_backward(
        dec_state, d_dec, dec_full, all_live, HEADS_D, images, patch_count
    )
    d_positions = d_dec_in.reshape(images, patch_count, dec_width)
    grad_mask = jnp.sum(jnp.where(shown_rows, 0.0, d_positions), axis=(0, 1))
    inverse = jnp.argsort(unshuffle, axis=1)[:, :slot_count]
    slot_live = (jnp.arange(slot_count, dtype=jnp.int32)[None, :] < visible[:, None])[:, :, None]
    d_embed = jnp.where(
        slot_live, jnp.take_along_axis(d_positions, inverse[:, :, None], axis=1), 0.0
    )
    d_embed_low = d_embed.reshape(images * slot_count, dec_width).astype(jnp.bfloat16)
    grad_embed = matmul_tn(enc_low, d_embed_low)
    d_enc = matmul_nt(d_embed_low, full_embed)
    d_rows_in, enc_grads = block_backward(
        enc_state, d_enc, enc_full, visible, HEADS, images, slot_count
    )

    vector_grads = (enc_grads[0], enc_grads[3], grad_mask, dec_grads[0], dec_grads[3])
    table = jnp.concatenate([g.reshape(members, -1) for g in vector_grads], axis=1)
    wide = 512 * -(-table.shape[1] // 512)
    table = jnp.pad(table, ((0, 0), (0, wide - table.shape[1])))
    table = jnp.broadcast_to(table[:, None, :], (members, 16, wide)).reshape(members * 16, wide)
    gradients = [
        item.astype(jnp.bfloat16)
        for item in (
            dec_grads[5],
            dec_grads[4],
            dec_grads[1],
            dec_grads[2],
            grad_embed,
            enc_grads[5],
            enc_grads[4],
            enc_grads[2],
            enc_grads[1],
            table,
        )
    ]
    if direct:
        sums = reduce_all(gradients, members // 2, 1)
    else:
        sums = reduce_plain(gradients)
    sums = [item.astype(jnp.float32) for item in sums]
    small = vectors_out(sums[9], sizes)
    return (
        enc_low.reshape(images, slot_count, model_width),
        dec_rows.astype(jnp.bfloat16).reshape(images, patch_count, dec_width),
        d_rows_in.astype(jnp.bfloat16).reshape(images, slot_count, model_width),
        small[0],
        sums[8],
        sums[7],
        small[1],
        sums[6],
        sums[5],
        sums[4],
        small[2],
        small[3],
        sums[2],
        sums[3],
        small[4],
        sums[1],
        sums[0],
    )


def solution(mesh):
    placed = (
        P(("rep", "fsdp"), None, None),
        P("fsdp"),
        P("fsdp", None),
        P("fsdp", None),
        P("fsdp"),
        P("fsdp", None),
        P("fsdp", None),
        P("fsdp", None),
        P("fsdp"),
        P("fsdp"),
        P("fsdp", None),
        P("fsdp", None),
        P("fsdp"),
        P("fsdp", None),
        P("fsdp", None),
        P(("rep", "fsdp")),
        P(("rep", "fsdp"), None),
        P(("rep", "fsdp")),
        P(("rep", "fsdp"), None, None),
    )
    return jax.shard_map(
        functools.partial(shards, dict(mesh.shape)),
        mesh=mesh,
        in_specs=placed,
        out_specs=(
            P(("rep", "fsdp"), None, None),
            P(("rep", "fsdp"), None, None),
            P(("rep", "fsdp"), None, None),
            P("fsdp"),
            P("fsdp", None),
            P("fsdp", None),
            P("fsdp"),
            P("fsdp", None),
            P("fsdp", None),
            P("fsdp", None),
            P("fsdp"),
            P("fsdp"),
            P("fsdp", None),
            P("fsdp", None),
            P("fsdp"),
            P("fsdp", None),
            P("fsdp", None),
        ),
        check_vma=False,
    )
```

```python
import functools

import jax
import jax.numpy as jnp
from jax import lax
from jax.experimental import pallas as pl
from jax.experimental.pallas import tpu as pltpu
from jax.sharding import PartitionSpec as P

HEADS = 16
HEADS_D = 16
GRID = 16


norm_epsilon = 1e-06
LOG2E = 1.4426950408889634


def matmul(left, right):
    return jnp.dot(left, right, preferred_element_type=jnp.float32)


def matmul_tn(left, right):
    return lax.dot_general(
        left, right, (((0,), (0,)), ((), ())), preferred_element_type=jnp.float32
    )


def matmul_nt(left, right):
    return lax.dot_general(
        left, right, (((1,), (1,)), ((), ())), preferred_element_type=jnp.float32
    )


def norm_stats(values):
    centre = values - jnp.mean(values, axis=-1, keepdims=True)
    inv_dev = lax.rsqrt(jnp.mean(centre * centre, axis=-1, keepdims=True) + norm_epsilon)
    return (centre * inv_dev, inv_dev)


def norm_back(d_scaled, normal, inv_dev):
    return inv_dev * (
        d_scaled
        - jnp.mean(d_scaled, axis=-1, keepdims=True)
        - normal * jnp.mean(d_scaled * normal, axis=-1, keepdims=True)
    )


def position_table(distance, grid_side, model_width):
    quarter = model_width // 4
    frequency = 1.0 / 10000.0 ** (jnp.arange(quarter, dtype=jnp.float32) / quarter)
    places = jnp.arange(grid_side * grid_side, dtype=jnp.int32)
    column = (places % grid_side).astype(jnp.float32)
    row_pos = (places // grid_side).astype(jnp.float32)
    along_c = distance[:, None, None] * column[None, :, None] * frequency[None, None, :]
    along_r = distance[:, None, None] * row_pos[None, :, None] * frequency[None, None, :]
    return jnp.concatenate(
        [jnp.sin(along_c), jnp.cos(along_c), jnp.sin(along_r), jnp.cos(along_r)], axis=-1
    )


def attend_kernel(width, heads, masked, live_ref, packed_ref, out_ref):
    size = width // heads
    length = packed_ref.shape[0]
    factor = size ** (-0.5) * LOG2E
    lanes = lax.broadcasted_iota(jnp.int32, (1, 128), 1) // size
    live = live_ref[pl.program_id(0)]

    @pl.loop(0, width // 128)
    def _(group):
        def part(index):
            start = pl.multiple_of(index * width + group * 128, 128)
            return packed_ref[:, pl.ds(start, 128)]

        queries, keys, values = part(0), part(1), part(2)
        total = None
        for head in range(128 // size):
            chosen = lanes == head
            scores = factor * matmul_nt(jnp.where(chosen, queries, 0), keys)
            if masked:
                column = lax.broadcasted_iota(jnp.int32, (1, length), 1)
                scores = jnp.where(column < live, scores, -1e30)
            exponent = jnp.exp2(scores - jnp.max(scores, axis=1, keepdims=True))
            inverse = 1.0 / jnp.sum(exponent, axis=1, keepdims=True)
            soft = (exponent * inverse).astype(jnp.bfloat16)
            mixed = matmul(soft, jnp.where(chosen, values, 0))
            total = mixed if total is None else total + mixed
        out_ref[:, pl.ds(pl.multiple_of(group * 128, 128), 128)] = total.astype(jnp.bfloat16)


def attend_back_kernel(width, heads, masked, live_ref, packed_ref, grad_ref, out_ref):
    size = width // heads
    length = packed_ref.shape[0]
    scale = size ** (-0.5)
    lanes = lax.broadcasted_iota(jnp.int32, (1, 128), 1) // size
    live = live_ref[pl.program_id(0)]

    @pl.loop(0, width // 128)
    def _(group):
        def place(index):
            return pl.ds(pl.multiple_of(index * width + group * 128, 128), 128)

        queries, keys, values = (packed_ref[:, place(index)] for index in range(3))
        d_mixed = grad_ref[:, place(0)]
        d_queries = d_keys = d_values = None
        for head in range(128 // size):
            chosen = lanes == head
            own_queries = jnp.where(chosen, queries, 0)
            own_grad = jnp.where(chosen, d_mixed, 0)
            own_keys = jnp.where(chosen, keys, 0)
            scores = (scale * LOG2E) * matmul_nt(keys, own_queries)
            if masked:
                row = lax.broadcasted_iota(jnp.int32, (length, 1), 0)
                scores = jnp.where(row < live, scores, -1e30)
            exponent = jnp.exp2(scores - jnp.max(scores, axis=0, keepdims=True))
            inverse = 1.0 / jnp.sum(exponent, axis=0, keepdims=True)
            soft = exponent * inverse
            d_soft = matmul_nt(values, own_grad)
            product = soft * d_soft
            column_dot = jnp.sum(product, axis=0, keepdims=True)
            d_scores = (product - soft * column_dot).astype(jnp.bfloat16)
            terms = (
                matmul_tn(d_scores, own_keys),
                matmul(d_scores, own_queries),
                matmul(soft.astype(jnp.bfloat16), own_grad),
            )
            if d_queries is None:
                d_queries, d_keys, d_values = terms
            else:
                d_queries, d_keys, d_values = (
                    d_queries + terms[0], d_keys + terms[1], d_values + terms[2],
                )
        out_ref[:, place(0)] = (d_queries * scale).astype(jnp.bfloat16)
        out_ref[:, place(1)] = (d_keys * scale).astype(jnp.bfloat16)
        out_ref[:, place(2)] = d_values.astype(jnp.bfloat16)


def attention_call(kernel, live, operands, width, wide, heads, masked):
    images = live.shape[0]
    length = operands[0].shape[0] // images
    pairs = images * heads * length * length
    return pl.pallas_call(
        functools.partial(kernel, width, heads, masked),
        out_shape=jax.ShapeDtypeStruct((images * length, wide), jnp.bfloat16),
        grid_spec=pltpu.PrefetchScalarGridSpec(
            num_scalar_prefetch=1,
            grid=(images,),
            in_specs=[
                pl.BlockSpec((length, item.shape[1]), lambda image, live: (image, 0))
                for item in operands
            ],
            out_specs=pl.BlockSpec((length, wide), lambda image, live: (image, 0)),
        ),
        compiler_params=pltpu.CompilerParams(vmem_limit_bytes=32 * 1024 * 1024),
        cost_estimate=pl.CostEstimate(
            flops=pairs * 1000,
            transcendentals=pairs,
            bytes_accessed=2 * images * length * (wide + 4 * width),
        ),
    )(live, *operands)


def block_forward(rows, weights, live, head_count, masked):
    gain_one, w_qkv, w_out, gain_two, w_up, w_down = weights
    model_width = rows.shape[-1]
    normal_one, inv_one = norm_stats(rows)
    normed_one = (normal_one * gain_one).astype(jnp.bfloat16)
    packed = matmul(normed_one, w_qkv).astype(jnp.bfloat16)
    mixed_rows = attention_call(
        attend_kernel, live, (packed,), model_width, model_width, head_count, masked
    )
    middle = rows + matmul(mixed_rows, w_out)
    normal_two, inv_two = norm_stats(middle)
    normed_two = (normal_two * gain_two).astype(jnp.bfloat16)
    hidden = jax.nn.gelu(matmul(normed_two, w_up), approximate=False).astype(jnp.bfloat16)
    return (middle + matmul(hidden, w_down), (rows, packed, mixed_rows, middle))


def block_backward(kept_state, d_out, weights, live, head_count, masked):
    rows, packed, mixed_rows, middle = kept_state
    gain_one, w_qkv, w_out, gain_two, w_up, w_down = weights
    model_width = rows.shape[-1]
    normal_two, inv_two = norm_stats(middle)
    normed_two = (normal_two * gain_two).astype(jnp.bfloat16)
    up_proj = matmul(normed_two, w_up)
    hidden_float, gelu_back = jax.vjp(lambda inner: jax.nn.gelu(inner, approximate=False), up_proj)
    hidden = hidden_float.astype(jnp.bfloat16)
    d_branch = d_out.astype(jnp.bfloat16)
    grad_down = matmul_tn(hidden, d_branch)
    d_hidden = matmul_nt(d_branch, w_down)
    d_up = gelu_back(d_hidden)[0].astype(jnp.bfloat16)
    grad_up = matmul_tn(normed_two, d_up)
    d_normed_two = matmul_nt(d_up, w_up)
    grad_gain_two = jnp.sum(d_normed_two * normal_two, axis=0)
    d_middle = d_out + norm_back(d_normed_two * gain_two, normal_two, inv_two)
    d_attn = d_middle.astype(jnp.bfloat16)
    grad_out = matmul_tn(mixed_rows, d_attn)
    d_mixed = matmul_nt(d_attn, w_out).astype(jnp.bfloat16)
    d_packed = attention_call(
        attend_back_kernel, live, (packed, d_mixed), model_width, 3 * model_width, head_count, masked
    )
    normal_one, inv_one = norm_stats(rows)
    normed_one = (normal_one * gain_one).astype(jnp.bfloat16)
    grad_qkv = matmul_tn(normed_one, d_packed)
    d_normed_one = matmul_nt(d_packed, w_qkv)
    grad_gain_one = jnp.sum(d_normed_one * normal_one, axis=0)
    d_rows = d_middle + norm_back(d_normed_one * gain_one, normal_one, inv_one)
    return (d_rows, (grad_gain_one, grad_qkv, grad_out, grad_gain_two, grad_up, grad_down))


MESH_ID = pl.DeviceIdType.MESH


def places():
    rep = lax.axis_index("rep")
    own = lax.axis_index("fsdp")
    return rep, own, own // 2, own % 2


def dev(rep, own):
    return {"rep": rep, "fsdp": own}


def greet(rep, own, line, length):
    barrier = pltpu.get_barrier_semaphore()

    def call(r, f):
        pl.semaphore_signal(barrier, inc=1, device_id=dev(r, f), device_id_type=MESH_ID)

    call(rep, own + 1 - 2 * (own % 2))
    call(rep + 1 - 2 * (rep % 2), own)
    call((rep + 2) % 4, own)

    @pl.when(line > 0)
    def _():
        call(rep, own - 2)

    @pl.when(line < length - 1)
    def _():
        call(rep, own + 2)

    ends = (line == 0).astype(jnp.int32) + (line == length - 1).astype(jnp.int32)
    pl.semaphore_wait(barrier, 5 - ends)


def gather_kernel(shapes, length, *refs):
    count = len(shapes)
    ins, outs, rest = (refs[:count], refs[count : 2 * count], refs[2 * count :])
    (own_sem, q_send, q_recv, o_send, z_send, z_recv, x_send, x_recv, y_send, y_recv) = rest[:10]
    d_send, d_recv, p_send, p_recv = rest[10:]
    rep, own, line, core = places()
    x_peer, y_peer = (rep + 1 - 2 * (rep % 2), (rep + 2) % 4)
    mate = own + 1 - 2 * core
    greet(rep, own, line, length)

    def window(k, source, quarter):
        rows, cols = shapes[k]
        start = pl.multiple_of((2 * source + core) * rows, 16)
        if quarter is None:
            return outs[k].at[pl.ds(start, rows), :]
        return outs[k].at[
            pl.ds(start, rows), pl.ds(pl.multiple_of(quarter * (cols // 4), 128), cols // 4)
        ]

    def send(src, dst, s_sem, r_sem, r, f):
        return pltpu.make_async_remote_copy(
            src_ref=src, dst_ref=dst, send_sem=s_sem, recv_sem=r_sem,
            device_id=dev(r, f), device_id_type=MESH_ID,
        )

    def mine(k):
        _, cols = shapes[k]
        return ins[k].at[:, pl.ds(pl.multiple_of(rep * (cols // 4), 128), cols // 4)]

    def left(k):
        return send(mine(k), window(k, line, rep), o_send.at[k, 0], z_recv.at[k, line], rep, own - 2)

    def right(k):
        return send(mine(k), window(k, line, rep), o_send.at[k, 1], z_recv.at[k, line], rep, own + 2)

    def start_own(k):
        @pl.when(line > 0)
        def _():
            left(k).start()

        @pl.when(line < length - 1)
        def _():
            right(k).start()

    def local(k):
        rows, _ = shapes[k]
        return pltpu.make_async_copy(
            ins[k], outs[k].at[pl.ds(pl.multiple_of(own * rows, 16), rows), :], own_sem.at[k]
        )

    def to_mate(k):
        rows, _ = shapes[k]
        return send(
            ins[k], outs[k].at[pl.ds(pl.multiple_of(own * rows, 16), rows), :],
            q_send.at[k], q_recv.at[k], rep, mate,
        )

    def z_step(k, s, sign):
        w = window(k, s, rep)
        return send(w, w, z_send.at[k, s], z_recv.at[k, s], rep, own - 2 * sign)

    def x_step(k, s):
        w = window(k, s, rep)
        return send(w, w, x_send.at[k, s], x_recv.at[k, s], x_peer, own)

    def y_step(k, s):
        w = window(k, s, rep)
        return send(w, w, y_send.at[k, s], y_recv.at[k, s], y_peer, own)

    def d_by_y(k, s):
        w = window(k, s, x_peer)
        return send(w, w, d_send.at[k, s], d_recv.at[k, s], y_peer, own)

    def d_by_x(k, s):
        w = window(k, s, y_peer)
        return send(w, w, d_send.at[k, s], d_recv.at[k, s], x_peer, own)

    def p_step(k, s):
        w = window(k, s, None)
        return send(w, w, p_send.at[k, s], p_recv.at[k, s], rep, mate)

    items = [(k, h, sign) for k in range(count) for h in range(1, length) for sign in (1, -1)]

    def each(item, body):
        k, h, sign = item
        s = line + sign * h
        if sign > 0:
            there, further = s < length, line > 0
        else:
            there, further = s >= 0, line < length - 1

        @pl.when(there)
        def _():
            body(k, s, sign, further)

    def stage_z(k, s, sign, further):
        z_step(k, s, sign).wait_recv()

        @pl.when(further)
        def _():
            z_step(k, s, sign).start()

        x_step(k, s).start()
        y_step(k, s).start()

    def stage_xy(k, s, sign, further):
        x_step(k, s).wait_recv()
        y_step(k, s).wait_recv()

        @pl.when((s + core) % 2 == 0)
        def _():
            d_by_y(k, s).start()

        @pl.when((s + core) % 2 == 1)
        def _():
            d_by_x(k, s).start()

    def stage_d(k, s, sign, further):
        d_by_x(k, s).wait_recv()
        p_step(k, s).start()

    def stage_end(k, s, sign, further):
        @pl.when(further)
        def _():
            z_step(k, s, sign).wait_send()

        x_step(k, s).wait_send()
        y_step(k, s).wait_send()
        d_by_x(k, s).wait_send()
        p_step(k, s).wait_send()
        p_step(k, s).wait_recv()

    start_own(0)
    if count > 1:
        start_own(1)
    for k in range(count):
        local(k).start()
        to_mate(k).start()
    lag, total = 6, len(items)
    for i in range(total + 2 * lag):
        if i < total:
            k, h, sign = items[i]
            if h == 1 and sign == 1 and k >= 1 and k + 1 < count:
                start_own(k + 1)
            each(items[i], stage_z)
        if 0 <= i - lag < total:
            each(items[i - lag], stage_xy)
        if 0 <= i - 2 * lag < total:
            each(items[i - 2 * lag], stage_d)
    for item in items:
        each(item, stage_end)
    for k in range(count):
        local(k).wait()
        to_mate(k).wait()

        @pl.when(line > 0)
        def _():
            left(k).wait_send()

        @pl.when(line < length - 1)
        def _():
            right(k).wait_send()


def gather_all(shards, length, ident):
    shapes = tuple(s.shape for s in shards)
    count = len(shapes)
    sem = pltpu.SemaphoreType.DMA
    return pl.pallas_call(
        functools.partial(gather_kernel, shapes, length),
        out_shape=tuple(
            jax.ShapeDtypeStruct((2 * length * rows, cols), jnp.bfloat16) for rows, cols in shapes
        ),
        in_specs=[pl.BlockSpec(memory_space=pltpu.VMEM)] * count,
        out_specs=tuple(pl.BlockSpec(memory_space=pl.ANY) for _ in shapes),
        scratch_shapes=[sem((count,)), sem((count,)), sem((count,)), sem((count, 2))]
        + [sem((count, length))] * 10,
        compiler_params=pltpu.CompilerParams(collective_id=ident, has_side_effects=True),
        name="gather_all",
    )(*shards)


def reduce_kernel(shapes, length, *refs):
    count = len(shapes)
    ins, outs, rest = (refs[:count], refs[count : 2 * count], refs[2 * count :])
    held, other, first, second, third, fourth = (
        rest[count * j : count * (j + 1)] for j in range(6)
    )
    rest = rest[6 * count :]
    (l_sem, p_send, p_recv, a_send, a_recv, b_send, b_recv, z_send, z_recv) = rest[:9]
    (w_recv, e_sem, f_send, f_recv, g_send, g_recv, h_send, h_recv) = rest[9:]
    rep, own, line, core = places()
    x_bit, y_bit = rep % 2, rep // 2
    x_peer, y_peer = (rep + 1 - 2 * x_bit, (rep + 2) % 4)
    mate = own + 1 - 2 * core
    greet(rep, own, line, length)

    def send(src, dst, s_sem, r_sem, r, f):
        return pltpu.make_async_remote_copy(
            src_ref=src, dst_ref=dst, send_sem=s_sem, recv_sem=r_sem,
            device_id=dev(r, f), device_id_type=MESH_ID,
        )

    def bits(t):
        if t % 2 == 0:
            return x_bit, y_bit, x_peer, y_peer
        return y_bit, x_bit, y_peer, x_peer

    def block(k, t, side):
        rows, _ = shapes[k]
        return ins[k].at[pl.ds(pl.multiple_of((2 * t + side) * rows, 16), rows), :]

    def load(k, t):
        return pltpu.make_async_copy(block(k, t, core), held[k].at[t], l_sem.at[k, t])

    def p_step(k, t):
        return send(
            block(k, t, 1 - core), other[k].at[t], p_send.at[k, t], p_recv.at[k, t], rep, mate
        )

    def cut(index, width):
        return pl.ds(pl.multiple_of(index * width, 128), width)

    def a_step(k, t):
        a, _, peer, _ = bits(t)
        half = shapes[k][1] // 2
        return send(
            held[k].at[t, :, cut(1 - a, half)], first[k].at[t],
            a_send.at[k, t], a_recv.at[k, t], peer, own,
        )

    def b_step(k, t):
        _, b, _, peer = bits(t)
        quarter = shapes[k][1] // 4
        return send(
            first[k].at[t, :, cut(1 - b, quarter)], second[k].at[t],
            b_send.at[k, t], b_recv.at[k, t], peer, own,
        )

    def z_right(k, t):
        if t == length:
            return None
        return send(second[k].at[t], third[k].at[t], z_send.at[k, t], z_recv.at[k, t], rep, own + 2)

    def z_left(k, t, last):
        dst, sem = (fourth[k], w_recv.at[k]) if last else (third[k].at[t], z_recv.at[k, t])
        return send(second[k].at[t], dst, z_send.at[k, t], sem, rep, own - 2)

    def add(k, rows, body):
        step = 16 if rows % 32 else 32

        @pl.loop(0, rows, step=step)
        def _(r):
            body(pl.ds(pl.multiple_of(r, 16), step))

    def stage_a(k, t):
        load(k, t).wait()
        p_step(k, t).wait_recv()

        def body(r):
            held[k][t, r, :] = held[k][t, r, :] + other[k][t, r, :]

        add(k, shapes[k][0], body)
        a_step(k, t).start()

    def stage_b(k, t):
        a, _, _, _ = bits(t)
        half = shapes[k][1] // 2
        a_step(k, t).wait_recv()

        def body(r):
            first[k][t, r, :] = first[k][t, r, :] + held[k][t, r, cut(a, half)]

        add(k, shapes[k][0], body)
        b_step(k, t).start()

    def stage_c(k, t):
        _, b, _, _ = bits(t)
        quarter = shapes[k][1] // 4
        b_step(k, t).wait_recv()

        def body(r):
            second[k][t, r, :] = second[k][t, r, :] + first[k][t, r, cut(b, quarter)]

        add(k, shapes[k][0], body)

    def join(k, t, source):
        def body(r):
            second[k][t, r, :] = second[k][t, r, :] + source[r, :]

        add(k, shapes[k][0], body)

    def stage_z(k, t, hop):
        if hop < t:

            @pl.when(line == hop)
            def _():
                if hop > 0:
                    z_right(k, t).wait_recv()
                    join(k, t, third[k].at[t])
                z_right(k, t).start()

        place = length - 1 - hop
        if place > t:

            @pl.when(line == place)
            def _():
                if hop > 0:
                    z_left(k, t, False).wait_recv()
                    join(k, t, third[k].at[t])
                z_left(k, t, place - 1 == t).start()

    def piece(k, t, flip_a, flip_b):
        a, b, _, _ = bits(t)
        a = 1 - a if flip_a else a
        b = 1 - b if flip_b else b
        return outs[k].at[:, cut(2 * a + b, shapes[k][1] // 4)]

    def put(k, t):
        return pltpu.make_async_copy(second[k].at[t], piece(k, t, 0, 0), e_sem.at[k])

    def f_step(k, t):
        return send(
            second[k].at[t], piece(k, t, 0, 0), f_send.at[k], f_recv.at[k], bits(t)[2], own
        )

    def g_step(k, t):
        return send(
            second[k].at[t], piece(k, t, 0, 0), g_send.at[k], g_recv.at[k], bits(t)[3], own
        )

    def h_first(k, t):
        w = piece(k, t, 0, 1)
        return send(w, w, h_send.at[k], h_recv.at[k], bits(t)[2], own)

    def h_second(k, t):
        w = piece(k, t, 1, 0)
        return send(w, w, h_send.at[k], h_recv.at[k], bits(t)[3], own)

    def stage_e(k, t):
        @pl.when(line == t)
        def _():
            if t > 0:
                z_right(k, t).wait_recv()
                join(k, t, third[k].at[t])
            if t < length - 1:
                z_left(k, t, True).wait_recv()
                join(k, t, fourth[k])
            put(k, t).start()
            f_step(k, t).start()
            g_step(k, t).start()

    def stage_f(k, t):
        @pl.when(line == t)
        def _():
            f_step(k, t).wait_recv()
            g_step(k, t).wait_recv()

            @pl.when(core == 0)
            def _():
                h_first(k, t).start()

            @pl.when(core == 1)
            def _():
                h_second(k, t).start()

    items = [(k, t) for k in range(count) for t in range(length)]
    for item in items:
        load(*item).start()
        p_step(*item).start()
    total, lag = len(items), 4
    plan = [(0, stage_a), (lag, stage_b), (2 * lag, stage_c)]
    for hop in range(length - 1):
        plan.append((3 * lag - 2 + hop * lag, functools.partial(stage_z, hop=hop)))
    plan.append((3 * lag - 2 + (length - 1) * lag, stage_e))
    plan.append((3 * lag - 2 + (length + 1) * lag, stage_f))
    for i in range(total + plan[-1][0]):
        for late, stage in plan:
            if 0 <= i - late < total:
                stage(*items[i - late])
    for k, t in items:
        p_step(k, t).wait_send()
        a_step(k, t).wait_send()
        b_step(k, t).wait_send()

        @pl.when(line < t)
        def _():
            z_right(k, t).wait_send()

        @pl.when(line > t)
        def _():
            z_left(k, t, False).wait_send()

        @pl.when(line == t)
        def _():
            put(k, t).wait()
            f_step(k, t).wait_send()
            g_step(k, t).wait_send()
            h_first(k, t).wait_send()
            h_first(k, t).wait_recv()


def reduce_all(arrays, length, ident):
    shapes = tuple((a.shape[0] // (2 * length), a.shape[1]) for a in arrays)
    count = len(shapes)
    sem = pltpu.SemaphoreType.DMA

    def room(part, lead=True):
        return [
            pltpu.VMEM(((length,) if lead else ()) + (rows, cols // part), jnp.bfloat16)
            for rows, cols in shapes
        ]

    return pl.pallas_call(
        functools.partial(reduce_kernel, shapes, length),
        out_shape=tuple(jax.ShapeDtypeStruct(s, jnp.bfloat16) for s in shapes),
        in_specs=[pl.BlockSpec(memory_space=pl.ANY)] * count,
        out_specs=tuple(pl.BlockSpec(memory_space=pl.ANY) for _ in shapes),
        scratch_shapes=room(1) + room(1) + room(2) + room(4) + room(4) + room(4, False)
        + [sem((count, length))] * 9
        + [sem((count,))] * 8,
        compiler_params=pltpu.CompilerParams(
            collective_id=ident, has_side_effects=True, vmem_limit_bytes=64 * 1024 * 1024 - 65536
        ),
        name="reduce_all",
    )(*arrays)


def vectors_in(vectors):
    flat = jnp.concatenate(vectors)
    wide = 512 * -(-flat.shape[0] // 512)
    flat = jnp.pad(flat, (0, wide - flat.shape[0]))
    return jnp.broadcast_to(flat[None, :], (16, wide))


def vectors_out(packed, sizes):
    table = packed.reshape(packed.shape[0] // 16, 16, packed.shape[1])[:, 0]
    results, offset = [], 0
    for size in sizes:
        results.append(table[:, offset : offset + size].reshape(-1))
        offset += size
    return results


def gather_plain(shards_of):
    return [lax.all_gather(shard, "fsdp", axis=0, tiled=True) for shard in shards_of]


def reduce_plain(arrays):
    return [
        lax.psum(lax.psum_scatter(array, "fsdp", scatter_dimension=0, tiled=True), "rep")
        for array in arrays
    ]


def shards(
    extents,
    patches,
    enc_gain1,
    enc_qkv,
    enc_proj,
    enc_gain2,
    enc_up,
    enc_down,
    embed_w,
    mask_token,
    dec_gain1,
    dec_qkv,
    dec_proj,
    dec_gain2,
    dec_up,
    dec_down,
    visible,
    unshuffle,
    ground_dist,
    cotangent,
):
    images, slot_count, model_width = patches.shape
    patch_count = unshuffle.shape[1]
    dec_width = embed_w.shape[1]
    members = extents["fsdp"]
    direct = members == 8 and extents["rep"] == 4

    vectors = (enc_gain1, enc_gain2, mask_token, dec_gain1, dec_gain2)
    sizes = [v.shape[0] for v in vectors]
    front = (vectors_in(vectors), enc_qkv, enc_proj, enc_up, enc_down, dec_proj)
    if direct:
        whole = gather_all(front, members // 2, 0)
    else:
        whole = gather_plain(front)
    full_gain1, full_gain2, full_mask, full_dec1, full_dec2 = vectors_out(whole[0], sizes)
    behind = lax.optimization_barrier((embed_w, dec_qkv, dec_up, dec_down, whole[0]))
    later = gather_plain(behind[:4])
    enc_full = (full_gain1, whole[1], whole[2], full_gain2, whole[3], whole[4])
    dec_full = (full_dec1, later[1], whole[5], full_dec2, later[2], later[3])
    full_embed = later[0]

    rows_in = patches.astype(jnp.float32).reshape(images * slot_count, model_width)
    enc_rows, enc_state = block_forward(rows_in, enc_full, visible, HEADS, True)
    enc_low = enc_rows.astype(jnp.bfloat16)
    embedded = matmul(enc_low, full_embed).reshape(images, slot_count, dec_width)
    picked = jnp.take_along_axis(
        embedded, jnp.minimum(unshuffle, slot_count - 1)[:, :, None], axis=1
    )
    shown_rows = (unshuffle < visible[:, None])[:, :, None]
    dec_in = jnp.where(
        shown_rows, picked, full_mask.astype(jnp.float32)[None, None, :]
    ) + position_table(ground_dist, GRID, dec_width)
    all_live = jnp.full((images,), patch_count, jnp.int32)
    dec_rows, dec_state = block_forward(
        dec_in.reshape(images * patch_count, dec_width),
        dec_full,
        all_live,
        HEADS_D,
        False,
    )
    d_dec = cotangent.astype(jnp.float32).reshape(images * patch_count, dec_width)
    d_dec_in, dec_grads = block_backward(
        dec_state, d_dec, dec_full, all_live, HEADS_D, False
    )
    d_positions = d_dec_in.reshape(images, patch_count, dec_width)
    grad_mask = jnp.sum(jnp.where(shown_rows, 0.0, d_positions), axis=(0, 1))
    inverse = jnp.argsort(unshuffle, axis=1)[:, :slot_count]
    slot_live = (jnp.arange(slot_count, dtype=jnp.int32)[None, :] < visible[:, None])[:, :, None]
    d_embed = jnp.where(
        slot_live, jnp.take_along_axis(d_positions, inverse[:, :, None], axis=1), 0.0
    )
    d_embed_low = d_embed.reshape(images * slot_count, dec_width).astype(jnp.bfloat16)
    grad_embed = matmul_tn(enc_low, d_embed_low)
    d_enc = matmul_nt(d_embed_low, full_embed)
    d_rows_in, enc_grads = block_backward(
        enc_state, d_enc, enc_full, visible, HEADS, True
    )

    vector_grads = (enc_grads[0], enc_grads[3], grad_mask, dec_grads[0], dec_grads[3])
    table = jnp.concatenate([g.reshape(members, -1) for g in vector_grads], axis=1)
    wide = 512 * -(-table.shape[1] // 512)
    table = jnp.pad(table, ((0, 0), (0, wide - table.shape[1])))
    table = jnp.broadcast_to(table[:, None, :], (members, 16, wide)).reshape(members * 16, wide)
    gradients = [
        item.astype(jnp.bfloat16)
        for item in (
            dec_grads[5],
            dec_grads[4],
            dec_grads[1],
            dec_grads[2],
            grad_embed,
            enc_grads[5],
            enc_grads[4],
            enc_grads[2],
            enc_grads[1],
            table,
        )
    ]
    if direct:
        sums = reduce_all(gradients, members // 2, 1)
    else:
        sums = reduce_plain(gradients)
    sums = [item.astype(jnp.float32) for item in sums]
    small = vectors_out(sums[9], sizes)
    return (
        enc_low.reshape(images, slot_count, model_width),
        dec_rows.astype(jnp.bfloat16).reshape(images, patch_count, dec_width),
        d_rows_in.astype(jnp.bfloat16).reshape(images, slot_count, model_width),
        small[0],
        sums[8],
        sums[7],
        small[1],
        sums[6],
        sums[5],
        sums[4],
        small[2],
        small[3],
        sums[2],
        sums[3],
        small[4],
        sums[1],
        sums[0],
    )


def solution(mesh):
    placed = (
        P(("rep", "fsdp"), None, None),
        P("fsdp"),
        P("fsdp", None),
        P("fsdp", None),
        P("fsdp"),
        P("fsdp", None),
        P("fsdp", None),
        P("fsdp", None),
        P("fsdp"),
        P("fsdp"),
        P("fsdp", None),
        P("fsdp", None),
        P("fsdp"),
        P("fsdp", None),
        P("fsdp", None),
        P(("rep", "fsdp")),
        P(("rep", "fsdp"), None),
        P(("rep", "fsdp")),
        P(("rep", "fsdp"), None, None),
    )
    return jax.shard_map(
        functools.partial(shards, dict(mesh.shape)),
        mesh=mesh,
        in_specs=placed,
        out_specs=(
            P(("rep", "fsdp"), None, None),
            P(("rep", "fsdp"), None, None),
            P(("rep", "fsdp"), None, None),
            P("fsdp"),
            P("fsdp", None),
            P("fsdp", None),
            P("fsdp"),
            P("fsdp", None),
            P("fsdp", None),
            P("fsdp", None),
            P("fsdp"),
            P("fsdp"),
            P("fsdp", None),
            P("fsdp", None),
            P("fsdp"),
            P("fsdp", None),
            P("fsdp", None),
        ),
        check_vma=False,
    )
```
